256 devices in a mesh: ctx: 32 (over x, y, core), tp: 8 (over z).
Axes of the slice: x: 4, y: 4, z: 8, core: 2. Of those that a mesh axis runs over, the one named last changes fastest.
Arguments:
- x_in: bfloat16 [16384, 8192], P('ctx', 'tp'), may hold values from -6 to 6
- gate_z: bfloat16 [16384, 8192], P('ctx', 'tp'), may hold values from -6 to 6
- b_in: bfloat16 [16384, 1024], P('ctx', 'tp'), may hold values from -1.5 to 1.5
- c_in: bfloat16 [16384, 1024], P('ctx', 'tp'), may hold values from -1.5 to 1.5
- step_size: float32 [16384, 128], P('ctx', 'tp'), may hold values from 0 to 2
- log_decay: float32 [16384, 128], P('ctx', 'tp'), may hold values from -1 to 0
- skip: float32 [128], P('tp'), may hold values from 0.5 to 2
- norm_gain: float32 [8192], P('tp'), may hold values from 0.1 to 1.9
- out_weight: bfloat16 [8192, 4096], P('tp'), may hold values from -0.0625 to 0.0625
Outputs:
- layer_out: bfloat16 [16384, 4096], P(('ctx', 'tp'))
The draws below stay inside these ranges and needn't reach their ends.
All inputs are finite; a program needn't handle non-finite values.
Results may differ from the reference program's by a relative error of at most 0.023.
Values may be sent and summed in bfloat16 or wider, within the bound.
A program may use at most 128 MiB of HBM per device.

```python
import math
from functools import partial
import jax
import jax.numpy as jnp
from jax import lax

HEADS = 128
HEAD_DIM = 64
STATE = 128
GROUPS = 8
DOUT = 4096
SPAN = 256
LEN_DEV = 512
DOCUMENT_TOKENS = 16384
DINNER = 8192
N_TP = 8


def fast_heads(key):
    share = 0.5
    return jax.random.uniform(jax.random.fold_in(key, 11), (HEADS,)) < share


def draw_log_decay(key, part):
    fast = fast_heads(key)
    keys = jax.random.split(jax.random.fold_in(key, 23), 6)
    fast_rate = jnp.exp(jax.random.uniform(keys[0], (HEADS,), jnp.float32, math.log(1.0 / 50.0), math.log(1.0 / 30.0)))
    slow_rate = jnp.exp(jax.random.uniform(keys[1], (HEADS,), jnp.float32, math.log(0.05), math.log(0.3))) / LEN_DEV
    speed_factor = jnp.where(fast, fast_rate, slow_rate)
    coarse_estimate = jnp.exp(jax.random.uniform(keys[2], (DOCUMENT_TOKENS, HEADS), jnp.float32, -0.5 * math.log(2.0), 0.5 * math.log(2.0)))
    zone_quantity = jnp.exp(jax.random.uniform(keys[3], (DOCUMENT_TOKENS // SPAN, 1), jnp.float32, -0.5 * math.log(2.0), 0.5 * math.log(2.0)))
    zone_quantity = jnp.repeat(zone_quantity, SPAN, axis=0)
    marked_locations = jax.random.randint(keys[4], (3,), 0, DOCUMENT_TOKENS)
    pulse_amplitude = jnp.any(jnp.arange(DOCUMENT_TOKENS)[:, None] == marked_locations[None, :], axis=1)
    layer_level = jax.random.uniform(keys[5], (DOCUMENT_TOKENS, HEADS), jnp.float32, math.log(1.25), math.log(2.0))
    return (-(speed_factor[None, :] * coarse_estimate * zone_quantity) - jnp.where(pulse_amplitude[:, None], layer_level, 0.0)).astype(jnp.float32)


def draw_step_size(key, part):
    fast = fast_heads(key)
    noise_key = jax.random.fold_in(key, 37)
    base = jnp.where(fast, 1.0, 2.0 / jnp.sqrt(jnp.float32(LEN_DEV)))
    coarse_estimate = jnp.exp(jax.random.uniform(noise_key, (DOCUMENT_TOKENS, HEADS), jnp.float32, -math.log(2.0), math.log(2.0)))
    return (base[None, :] * coarse_estimate).astype(jnp.float32)


def levels(rng, shape, cuts, least, high):
    level = 1.0
    for position, parts in cuts:
        heights = jax.random.uniform(jax.random.fold_in(jax.random.fold_in(rng, 6), position), (parts,), jnp.float32, least / len(cuts), high / len(cuts))
        level = level * jnp.repeat(jnp.exp(heights), shape[position] // parts).reshape((-1,) + (1,) * (len(shape) - 1 - position))
    return level


def gaussian(stream_key, dims, scale, most, pieces=(), kind=jnp.bfloat16):
    drawn = scale * jax.random.normal(stream_key, dims, jnp.float32)
    if pieces:
        drawn = drawn * levels(stream_key, dims, pieces, -0.22, 0.18)
    return jnp.clip(drawn, -most, most).astype(kind)


def setup_inputs(seed: int = 0) -> dict:
    splits = jax.random.split(jax.random.key(seed), 10)
    x_in = gaussian(splits[0], (DOCUMENT_TOKENS, DINNER), 1.0, 6.0, ((0, 32), (1, 8)))
    gate_z = gaussian(splits[1], (DOCUMENT_TOKENS, DINNER), 1.0, 6.0, ((0, 32), (1, 8)))
    b_in = gaussian(splits[2], (DOCUMENT_TOKENS, GROUPS * STATE), 0.25, 1.5, ((0, 32), (1, 8)))
    c_in = gaussian(splits[3], (DOCUMENT_TOKENS, GROUPS * STATE), 0.25, 1.5, ((0, 32), (1, 8)))
    step_size = draw_step_size(jax.random.fold_in(splits[9], 71), 0)
    log_decay = draw_log_decay(jax.random.fold_in(splits[9], 71), 0)
    skip = jnp.clip(0.5 + 1.5 * jax.random.uniform(splits[6], (HEADS,), jnp.float32) ** levels(splits[6], (HEADS,), ((0, 8),), -0.2, 0.2), 0.5, 2.0)
    norm_gain = jnp.clip(1.0 + 0.18 * jax.random.normal(splits[7], (DINNER,), jnp.float32), 0.1, 1.9)
    out_weight = gaussian(splits[8], (DINNER, DOUT), DINNER ** -0.5, 0.0625, ((0, 8),))
    return {"x_in": x_in, "gate_z": gate_z, "b_in": b_in, "c_in": c_in, "step_size": step_size, "log_decay": log_decay, "skip": skip, "norm_gain": norm_gain, "out_weight": out_weight}


def block_pass(states, inputs, per_group):
    scaled, decay_log, b_block, c_block = inputs
    block_len = decay_log.shape[0]
    head_count = decay_log.shape[1]
    group_count = b_block.shape[1]
    running = jnp.cumsum(decay_log, axis=0)
    b_wide = b_block.astype(jnp.float32)
    c_wide = c_block.astype(jnp.float32)
    scores = jnp.einsum('tgn,sgn->gts', c_wide, b_wide, precision=lax.Precision.HIGHEST)
    scores = jnp.repeat(scores, per_group, axis=0)
    run_heads = running.T
    spread = run_heads[:, :, None] - run_heads[:, None, :]
    causal = lax.broadcasted_iota(jnp.int32, (block_len, block_len), 0) >= lax.broadcasted_iota(jnp.int32, (block_len, block_len), 1)
    decays = jnp.where(causal[None], jnp.exp(jnp.where(causal[None], spread, 0.0)), 0.0)
    weights = scores * decays
    within = jnp.einsum('hts,shp->thp', weights, scaled, precision=lax.Precision.HIGHEST)
    grouped = states.reshape(group_count, per_group, states.shape[1], states.shape[2])
    carried = jnp.einsum('tgn,gkpn->tgkp', c_wide, grouped, precision=lax.Precision.HIGHEST)
    carried = carried.reshape(block_len, head_count, states.shape[1]) * jnp.exp(running)[:, :, None]
    tail_decay = jnp.exp(running[-1][None, :] - running)
    weighted = (scaled * tail_decay[:, :, None]).reshape(block_len, group_count, per_group, states.shape[1])
    fresh_in = jnp.einsum('sgn,sgkp->gkpn', b_wide, weighted, precision=lax.Precision.HIGHEST)
    new_states = states * jnp.exp(running[-1])[:, None, None] + fresh_in.reshape(states.shape)
    return (new_states, within + carried)

def reference(x_in, gate_z, b_in, c_in, step_size, log_decay, skip, norm_gain, out_weight):
    total_rows = x_in.shape[0]
    blocks = total_rows // SPAN
    per_group = HEADS // GROUPS
    inputs = x_in.astype(jnp.float32).reshape(total_rows, HEADS, HEAD_DIM)
    scaled = inputs * step_size[:, :, None]
    b_groups = b_in.reshape(blocks, SPAN, GROUPS, STATE)
    c_groups = c_in.reshape(blocks, SPAN, GROUPS, STATE)
    start_state = jnp.zeros((HEADS, HEAD_DIM, STATE), jnp.float32)
    final_state, outputs = lax.scan(partial(block_pass, per_group=per_group), start_state, (scaled.reshape(blocks, SPAN, HEADS, HEAD_DIM), log_decay.reshape(blocks, SPAN, HEADS), b_groups, c_groups))
    outputs = outputs.reshape(total_rows, HEADS, HEAD_DIM)
    mixed = (outputs + skip[None, :, None] * inputs).reshape(total_rows, DINNER)
    mixed = mixed * jax.nn.silu(gate_z.astype(jnp.float32))
    by_group = mixed.reshape(total_rows, GROUPS, DINNER // GROUPS)
    meansq = lax.optimization_barrier(jnp.mean(by_group * by_group, axis=2, keepdims=True))
    normed = ((by_group * lax.rsqrt(meansq + 1e-05)).reshape(total_rows, DINNER) * norm_gain[None, :]).astype(jnp.bfloat16)
    split = DINNER // N_TP

    def add_block(total, block_index):
        piece = lax.dynamic_slice_in_dim(normed, block_index * split, split, 1)
        rows_block = lax.dynamic_slice_in_dim(out_weight, block_index * split, split, 0)
        partial_sum = jnp.dot(piece, rows_block, preferred_element_type=jnp.float32)
        rounded = lax.optimization_barrier(partial_sum.astype(jnp.bfloat16))
        return (total + rounded.astype(jnp.float32), None)
    summed, unused = lax.scan(add_block, jnp.zeros((total_rows, DOUT), jnp.float32), jnp.arange(N_TP, dtype=jnp.int32))
    return summed.astype(jnp.bfloat16)
```

```python
import jax
import jax.numpy as jnp
from jax import lax
from jax.experimental import pallas as pl
from jax.experimental.pallas import tpu as pltpu
from jax.sharding import PartitionSpec as P

F32 = jnp.float32
BF16 = jnp.bfloat16
HEADS = 16
HEAD_DIM = 64
STATE = 128
CHUNK = 128
ROWS = 512
CHAN = 1024
HALF = CHAN // 2
DOUT = 4096
TP = 8
BLOCK = ROWS // TP
SIDE = DOUT // 2
SUB = 2
SUBW = SIDE // SUB
TILE = 512
LEVELS = 4
PIECES = 2
PROWS = STATE // PIECES
HEAD_ROWS = 16


def iota(shape, dim):
    return lax.broadcasted_iota(jnp.int32, shape, dim)


def split2(v):
    high = v.astype(BF16)
    return high, (v - high.astype(F32)).astype(BF16)


def nn(a, b):
    return lax.dot_general(a, b, (((1,), (0,)), ((), ())), preferred_element_type=F32)


def nt(a, b):
    return lax.dot_general(a, b, (((1,), (1,)), ((), ())), preferred_element_type=F32)


def tn(a, b):
    return lax.dot_general(a, b, (((0,), (0,)), ((), ())), preferred_element_type=F32)


def per_channel(by_head, expand):
    return tn(jnp.concatenate(split2(by_head), axis=0), expand)


def decay_rows(row):
    high, low = split2(row)
    shape = (HEAD_ROWS // 2, row.shape[1])
    both = [jnp.broadcast_to(v.astype(F32), shape) for v in (high, low)]
    return jnp.concatenate(both, axis=0).astype(BF16)


def decay_of(tile):
    tile = tile.astype(F32)
    return tile[0:1] + tile[HEAD_ROWS // 2 : HEAD_ROWS // 2 + 1]


def kernel(
    x_ref, b_ref, dt_ref, ld_ref, skip_ref, gain_ref, z_hbm, c_ref, w_hbm,
    o_ref,
    z_ref, w_ref, wa_ref, wb_ref, sc_ref, us_ref, s_ref, sloc_ref, ga_ref, gx_ref,
    e_send, e_recv, lv_send, lv_recv, t_ref, p_ref, pre_send, pre_recv,
    n_ref, pr_ref, rs_send, rs_recv,
    z_sem, w_sem, e_ss, e_rs, lv_ss, lv_rs, pre_ss, pre_rs, rs_ss, rs_rs,
):
    ctx = lax.axis_index("ctx")
    z = lax.axis_index("tp")
    core = lax.rem(ctx, 2)
    y = lax.rem(lax.div(ctx, 2), 4)
    x = lax.div(ctx, 8)
    peer = ctx + 1 - 2 * core
    partners = [
        ctx + 2 * (1 - 2 * lax.rem(y, 2)),
        ctx + 2 * (3 - 2 * y),
        ctx + 8 * (1 - 2 * lax.rem(x, 2)),
        ctx + 8 * (3 - 2 * x),
    ]
    later = [lax.rem(y, 2), lax.div(y, 2), lax.rem(x, 2), lax.div(x, 2)]
    ring = [lax.rem(z + 1, TP), lax.rem(z + TP - 1, TP)]
    mine = pl.multiple_of(core * HALF, HALF)
    other = pl.multiple_of((1 - core) * HALF, HALF)

    barrier = pltpu.get_barrier_semaphore()
    for c in [peer] + partners:
        pl.semaphore_signal(barrier, inc=1, device_id={"ctx": c}, device_id_type=pl.DeviceIdType.MESH)
    for t in ring:
        pl.semaphore_signal(barrier, inc=1, device_id={"tp": t}, device_id_type=pl.DeviceIdType.MESH)

    z_copy = pltpu.make_async_copy(z_hbm, z_ref, z_sem)
    z_copy.start()
    w_copy = pltpu.make_async_copy(w_hbm, w_ref, w_sem)
    w_copy.start()

    lane = iota((HEADS, CHAN), 1)
    first = iota((HEADS, CHAN), 0) * HEAD_DIM
    one_head = jnp.where((lane >= first) & (lane < first + HEAD_DIM), 1.0, 0.0).astype(BF16)
    expand = jnp.concatenate([one_head, one_head], axis=0)
    upper = jnp.where(iota((CHUNK, CHUNK), 0) <= iota((CHUNK, CHUNK), 1), 1.0, 0.0).astype(BF16)

    chunks = ROWS // CHUNK

    def stack(ref):
        return jnp.concatenate([ref[:, k * CHUNK : (k + 1) * CHUNK] for k in range(chunks)], axis=0)

    log_decay = stack(ld_ref)
    high, low = split2(log_decay)
    rest = ((log_decay - high.astype(F32)) - low.astype(F32)).astype(BF16)
    run = nn(high, upper) + nn(low, upper) + nn(rest, upper)
    middle = jnp.broadcast_to(run[:, CHUNK // 2 - 1 : CHUNK // 2], run.shape)
    total = jnp.broadcast_to(run[:, CHUNK - 1 : CHUNK], run.shape)
    wa_ref[...] = jnp.exp(run - middle)
    wb_ref[...] = jnp.exp(middle - run) * stack(dt_ref)
    column = iota((HEADS, CHUNK), 1)
    logs = jnp.zeros((HEADS, CHUNK), F32)
    before = jnp.zeros((HEADS, CHUNK), F32)
    for k in range(chunks):
        mid_k = middle[k * HEADS : (k + 1) * HEADS]
        tot_k = total[k * HEADS : (k + 1) * HEADS]
        logs = jnp.where(column == k, tot_k - mid_k, logs)
        logs = jnp.where(column == 4 + k, mid_k, logs)
        logs = jnp.where(column == 8 + k, tot_k, logs)
        logs = jnp.where(column == 12 + k, before, logs)
        before = before + tot_k
    logs = jnp.where(column == 16, before, logs)
    sc_ref[...] = per_channel(jnp.exp(logs), expand)[0:32]
    s_ref[...] = jnp.zeros_like(s_ref)

    def local_chunk(k, carry):
        rows = pl.ds(pl.multiple_of(k * CHUNK, CHUNK), CHUNK)
        heads = pl.ds(pl.multiple_of(k * HEADS, HEADS), HEADS)
        factor = per_channel(wb_ref[heads, :], expand)
        u = (x_ref[rows, :].astype(F32) * factor).astype(BF16)
        us_ref[pl.ds(pl.multiple_of(k * 2 * CHUNK, CHUNK), CHUNK), :] = u
        fresh = tn(b_ref[rows, :], u)
        state = s_ref[...]
        sloc_ref[pl.ds(pl.multiple_of(k * STATE, STATE), STATE), :] = state
        s_ref[...] = sc_ref[pl.ds(8 + k, 1), :] * state + sc_ref[pl.ds(k, 1), :] * fresh
        return carry

    lax.fori_loop(0, chunks, local_chunk, 0)

    pl.semaphore_wait(barrier, 7)

    def to_peer(h, slot):
        return pltpu.make_async_remote_copy(
            src_ref=e_send.at[h], dst_ref=e_recv.at[h], send_sem=e_ss.at[slot], recv_sem=e_rs.at[slot],
            device_id={"ctx": peer}, device_id_type=pl.DeviceIdType.MESH,
        )

    e_copies = []
    for slot, (h, lanes) in enumerate([(1 - core, pl.ds(other, HALF)), (core, pl.ds(mine, HALF))]):
        e_send[h, 0:HEAD_ROWS, :] = decay_rows(sc_ref[16:17, lanes])
        e_send[h, HEAD_ROWS:, :] = s_ref[:, lanes].astype(BF16)
        copy = to_peer(h, slot)
        copy.start()
        e_copies.append(copy)

    skip_row = nn(jnp.concatenate(split2(skip_ref[...]), axis=1), expand)

    def gate(k):
        rows = slice(k * CHUNK, (k + 1) * CHUNK)
        after = per_channel(wa_ref[k * HEADS : (k + 1) * HEADS, :], expand)
        v = z_ref[rows, :].astype(F32)
        gated = v / (1.0 + jnp.exp(-v))
        ga_ref[rows, :] = after * gated
        gx_ref[rows, :] = skip_row * x_ref[rows, :].astype(F32) * gated

    to_peer(core, 0).wait_recv()
    is_late = core == 1
    d_mine = sc_ref[16:17, pl.ds(mine, HALF)]
    d_peer = decay_of(e_recv[core, 0:HEAD_ROWS, :])
    block_decay = d_mine * d_peer
    scale_mine = jnp.where(is_late, 1.0, d_peer)
    scale_peer = jnp.where(is_late, d_mine, 1.0)

    def level_copy(l, p):
        rows = slice(0 if p == 0 else HEAD_ROWS + p * PROWS, HEAD_ROWS + (p + 1) * PROWS)
        return pltpu.make_async_remote_copy(
            src_ref=lv_send.at[l, rows, :], dst_ref=lv_recv.at[l, rows, :],
            send_sem=lv_ss.at[l, p], recv_sem=lv_rs.at[l, p],
            device_id={"ctx": partners[l]}, device_id_type=pl.DeviceIdType.MESH,
        )

    def send_level(l, p, state, decay):
        if p == 0:
            lv_send[l, 0:HEAD_ROWS, :] = decay_rows(decay)
        lv_send[l, HEAD_ROWS + p * PROWS : HEAD_ROWS + (p + 1) * PROWS, :] = state.astype(BF16)
        level_copy(l, p).start()

    for p in range(PIECES):
        rows = slice(p * PROWS, (p + 1) * PROWS)
        theirs = e_recv[core, HEAD_ROWS + p * PROWS : HEAD_ROWS + (p + 1) * PROWS, :].astype(F32)
        state = scale_mine * s_ref[rows, pl.ds(mine, HALF)] + scale_peer * theirs
        t_ref[rows, :] = state
        send_level(0, p, state, block_decay)

    z_copy.wait()
    prefix_decay = jnp.ones((1, HALF), F32)
    for l in range(LEVELS):
        gate(l)
        up = later[l] == 1
        for p in range(PIECES):
            rows = slice(p * PROWS, (p + 1) * PROWS)
            level_copy(l, p).wait_recv()
            if p == 0:
                their_decay = decay_of(lv_recv[l, 0:HEAD_ROWS, :])
                to_prefix = jnp.where(up, prefix_decay, 0.0)
                scale_theirs = jnp.where(up, block_decay, 1.0)
                scale_ours = jnp.where(up, 1.0, their_decay)
                next_decay = block_decay * their_decay
            theirs = lv_recv[l, HEAD_ROWS + p * PROWS : HEAD_ROWS + (p + 1) * PROWS, :].astype(F32)
            if l < LEVELS - 1:
                state = scale_theirs * theirs + scale_ours * t_ref[rows, :]
                t_ref[rows, :] = state
                send_level(l + 1, p, state, next_decay)
            gain = to_prefix * theirs
            prefix = gain if l == 0 else p_ref[rows, :] + gain
            if l < LEVELS - 1:
                p_ref[rows, :] = prefix
            else:
                pre_send[rows, :] = prefix.astype(BF16)
        prefix_decay = jnp.where(up, prefix_decay * their_decay, prefix_decay)
        block_decay = next_decay

    pre_copy = pltpu.make_async_remote_copy(
        src_ref=pre_send, dst_ref=pre_recv, send_sem=pre_ss, recv_sem=pre_rs,
        device_id={"ctx": peer}, device_id_type=pl.DeviceIdType.MESH,
    )
    pre_copy.start()
    to_peer(1 - core, 1).wait_recv()

    def finish(h, lanes, ref):
        theirs = e_recv[h, HEAD_ROWS:, :].astype(F32)
        decay = decay_of(e_recv[h, 0:HEAD_ROWS, :])
        start = jnp.where(is_late, decay, 1.0) * ref[...].astype(F32) + jnp.where(is_late, theirs, 0.0)
        for k in range(chunks):
            state = sloc_ref[k * STATE : (k + 1) * STATE, lanes] + sc_ref[12 + k : 13 + k, lanes] * start
            rows = slice((2 * k + 1) * CHUNK, (2 * k + 2) * CHUNK)
            us_ref[rows, lanes] = (sc_ref[4 + k : 5 + k, lanes] * state).astype(BF16)

    finish(core, pl.ds(mine, HALF), pre_send)
    pre_copy.wait_recv()
    finish(1 - core, pl.ds(other, HALF), pre_recv)

    def norm_block(i, carry):
        away = lax.div(i, 2) + 1
        step = jnp.where(i == TP - 1, 0, away * (2 * lax.rem(i, 2) - 1))
        block = lax.rem(z + step + TP, TP)
        k = lax.div(block, 2)
        rows = pl.ds(pl.multiple_of(block * BLOCK, BLOCK), BLOCK)
        c = c_ref[rows, :]
        scores = nt(c, b_ref[pl.ds(pl.multiple_of(k * CHUNK, CHUNK), CHUNK), :])
        t = lax.rem(block, 2) * BLOCK + iota((BLOCK, CHUNK), 0)
        scores = jnp.where(t >= iota((BLOCK, CHUNK), 1), scores, 0.0).astype(BF16)
        ssm = nn(jnp.concatenate([scores, c], axis=1), us_ref[pl.ds(pl.multiple_of(k * 2 * CHUNK, CHUNK), 2 * CHUNK), :])
        mixed = ssm * ga_ref[rows, :] + gx_ref[rows, :]
        meansq = jnp.sum(mixed * mixed, axis=1, keepdims=True) * (1.0 / CHAN)
        n_ref[rows, :] = (mixed * lax.rsqrt(meansq + 1e-05) * gain_ref[...]).astype(BF16)
        return carry

    def block_of(d, step):
        return lax.rem(z + (1 + step if d else 2 * TP - 1 - step), TP)

    def project(q):
        slot = q % 2
        for d in range(2):
            pair = jnp.concatenate(
                [n_ref[pl.ds(pl.multiple_of(block_of(d, s) * BLOCK, BLOCK), BLOCK), :] for s in (2 * q, 2 * q + 1)],
                axis=0,
            )

            def tile(j, carry):
                here = pl.ds(pl.multiple_of(j * TILE, TILE), TILE)
                there = pl.ds(pl.multiple_of(d * SIDE + j * TILE, TILE), TILE)
                pr_ref[slot, d, :, here] = nn(pair, w_ref[:, there])
                return carry

            lax.fori_loop(0, SIDE // TILE, tile, 0)

    def ring_copy(s, d, j):
        return pltpu.make_async_remote_copy(
            src_ref=rs_send.at[s, d, j], dst_ref=rs_recv.at[s, d, j],
            send_sem=rs_ss.at[s, d, j], recv_sem=rs_rs.at[s, d, j],
            device_id={"tp": ring[d]}, device_id_type=pl.DeviceIdType.MESH,
        )

    def ring_step(s):
        slot = (s // 2) % 2
        rows = slice((s % 2) * BLOCK, (s % 2 + 1) * BLOCK)
        for j in range(SUB):
            for d in range(2):
                value = pr_ref[slot, d, rows, j * SUBW : (j + 1) * SUBW]
                if s > 0:
                    ring_copy(s - 1, d, j).wait_recv()
                    value = value + rs_recv[s - 1, d, j].astype(F32)
                if s < TP - 1:
                    rs_send[s, d, j] = value.astype(BF16)
                    ring_copy(s, d, j).start()
                else:
                    o_ref[:, d * SIDE + j * SUBW : d * SIDE + (j + 1) * SUBW] = value.astype(BF16)

    lax.fori_loop(0, 4, norm_block, 0)
    w_copy.wait()
    project(0)
    for q in range(TP // 2):
        ring_step(2 * q)
        if q == 0:
            lax.fori_loop(4, TP, norm_block, 0)
        if q < TP // 2 - 1:
            project(q + 1)
        ring_step(2 * q + 1)

    for copy in e_copies:
        copy.wait_send()
    pre_copy.wait_send()
    for l in range(LEVELS):
        for p in range(PIECES):
            level_copy(l, p).wait_send()
    for s in range(TP - 1):
        for d in range(2):
            for j in range(SUB):
                ring_copy(s, d, j).wait_send()


def on_device(x_in, gate_z, b_in, c_in, step_size, log_decay, skip, norm_gain, out_weight):
    vmem = pl.BlockSpec(memory_space=pltpu.VMEM)
    anywhere = pl.BlockSpec(memory_space=pl.ANY)
    dma = pltpu.SemaphoreType.DMA
    return pl.pallas_call(
        kernel,
        out_shape=jax.ShapeDtypeStruct((BLOCK, DOUT), BF16),
        in_specs=[vmem] * 6 + [anywhere, vmem, anywhere],
        out_specs=vmem,
        scratch_shapes=[
            pltpu.VMEM((ROWS, CHAN), BF16),
            pltpu.VMEM((CHAN, DOUT), BF16),
            pltpu.VMEM((64, CHUNK), F32),
            pltpu.VMEM((64, CHUNK), F32),
            pltpu.VMEM((32, CHAN), F32),
            pltpu.VMEM((2 * ROWS, CHAN), BF16),
            pltpu.VMEM((STATE, CHAN), F32),
            pltpu.VMEM((4 * STATE, CHAN), F32),
            pltpu.VMEM((ROWS, CHAN), F32),
            pltpu.VMEM((ROWS, CHAN), F32),
            pltpu.VMEM((2, HEAD_ROWS + STATE, HALF), BF16),
            pltpu.VMEM((2, HEAD_ROWS + STATE, HALF), BF16),
            pltpu.VMEM((LEVELS, HEAD_ROWS + STATE, HALF), BF16),
            pltpu.VMEM((LEVELS, HEAD_ROWS + STATE, HALF), BF16),
            pltpu.VMEM((STATE, HALF), F32),
            pltpu.VMEM((STATE, HALF), F32),
            pltpu.VMEM((STATE, HALF), BF16),
            pltpu.VMEM((STATE, HALF), BF16),
            pltpu.VMEM((ROWS, CHAN), BF16),
            pltpu.VMEM((2, 2, 2 * BLOCK, SIDE), F32),
            pltpu.VMEM((TP - 1, 2, SUB, BLOCK, SUBW), BF16),
            pltpu.VMEM((TP - 1, 2, SUB, BLOCK, SUBW), BF16),
            dma, dma,
            dma((2,)), dma((2,)),
            dma((LEVELS, PIECES)), dma((LEVELS, PIECES)),
            dma, dma,
            dma((TP - 1, 2, SUB)), dma((TP - 1, 2, SUB)),
        ],
        compiler_params=pltpu.CompilerParams(
            collective_id=0, has_side_effects=True, vmem_limit_bytes=56 * 1024 * 1024
        ),
        name="state_space_layer",
    )(
        x_in, b_in, step_size.T, log_decay.T, skip.reshape(1, HEADS), norm_gain.reshape(1, CHAN), gate_z, c_in, out_weight,
    )


def solution(mesh):
    placed = (
        P("ctx", "tp"),
        P("ctx", "tp"),
        P("ctx", "tp"),
        P("ctx", "tp"),
        P("ctx", "tp"),
        P("ctx", "tp"),
        P("tp"),
        P("tp"),
        P("tp", None),
    )
    return jax.shard_map(
        on_device, mesh=mesh, in_specs=placed, out_specs=P(("ctx", "tp"), None), check_vma=False
    )
```

```python
import jax
import jax.numpy as jnp
from jax import lax
from jax.experimental import pallas as pl
from jax.experimental.pallas import tpu as pltpu
from jax.sharding import PartitionSpec as P

F32 = jnp.float32
BF16 = jnp.bfloat16
HEADS = 16
HEAD_DIM = 64
STATE = 128
CHUNK = 128
ROWS = 512
CHAN = 1024
HALF = CHAN // 2
DOUT = 4096
TP = 8
BLOCK = ROWS // TP
SIDE = DOUT // 2
SUB = 4
SUBW = SIDE // SUB
LEVELS = 4
PIECES = 8
PROWS = STATE // PIECES
HEAD_ROWS = 16


def iota(shape, dim):
    return lax.broadcasted_iota(jnp.int32, shape, dim)


def split2(v):
    high = v.astype(BF16)
    return high, (v - high.astype(F32)).astype(BF16)


def nn(a, b):
    return lax.dot_general(a, b, (((1,), (0,)), ((), ())), preferred_element_type=F32)


def nt(a, b):
    return lax.dot_general(a, b, (((1,), (1,)), ((), ())), preferred_element_type=F32)


def tn(a, b):
    return lax.dot_general(a, b, (((0,), (0,)), ((), ())), preferred_element_type=F32)


def per_channel(by_head, expand):
    return tn(jnp.concatenate(split2(by_head), axis=0), expand)


def decay_rows(row):
    high, low = split2(row)
    shape = (HEAD_ROWS // 2, row.shape[1])
    both = [jnp.broadcast_to(v.astype(F32), shape) for v in (high, low)]
    return jnp.concatenate(both, axis=0).astype(BF16)


def decay_of(tile):
    tile = tile.astype(F32)
    return tile[0:1] + tile[HEAD_ROWS // 2 : HEAD_ROWS // 2 + 1]


def kernel(
    x_ref, b_ref, dt_ref, ld_ref, skip_ref, gain_ref, z_hbm, c_ref, w_hbm,
    o_ref,
    z_ref, w_ref, wa_ref, wb_ref, sc_ref, us_ref, s_ref, sloc_ref, ga_ref, gx_ref,
    e_send, e_recv, lv_send, lv_recv, t_ref, p_ref, pre_send, pre_recv,
    n_ref, pr_ref, rs_send, rs_recv,
    z_sem, w_sem, e_ss, e_rs, lv_ss, lv_rs, pre_ss, pre_rs, rs_ss, rs_rs,
):
    ctx = lax.axis_index("ctx")
    z = lax.axis_index("tp")
    core = lax.rem(ctx, 2)
    y = lax.rem(lax.div(ctx, 2), 4)
    x = lax.div(ctx, 8)
    peer = ctx + 1 - 2 * core
    partners = [
        ctx + 2 * (1 - 2 * lax.rem(y, 2)),
        ctx + 2 * (3 - 2 * y),
        ctx + 8 * (1 - 2 * lax.rem(x, 2)),
        ctx + 8 * (3 - 2 * x),
    ]
    later = [lax.rem(y, 2), lax.div(y, 2), lax.rem(x, 2), lax.div(x, 2)]
    ring = [lax.rem(z + 1, TP), lax.rem(z + TP - 1, TP)]
    mine = pl.multiple_of(core * HALF, HALF)
    other = pl.multiple_of((1 - core) * HALF, HALF)

    barrier = pltpu.get_barrier_semaphore()
    for c in [peer] + partners:
        pl.semaphore_signal(barrier, inc=1, device_id={"ctx": c}, device_id_type=pl.DeviceIdType.MESH)
    for t in ring:
        pl.semaphore_signal(barrier, inc=1, device_id={"tp": t}, device_id_type=pl.DeviceIdType.MESH)

    z_copy = pltpu.make_async_copy(z_hbm, z_ref, z_sem)
    z_copy.start()
    w_copy = pltpu.make_async_copy(w_hbm, w_ref, w_sem)
    w_copy.start()

    lane = iota((HEADS, CHAN), 1)
    first = iota((HEADS, CHAN), 0) * HEAD_DIM
    one_head = jnp.where((lane >= first) & (lane < first + HEAD_DIM), 1.0, 0.0).astype(BF16)
    expand = jnp.concatenate([one_head, one_head], axis=0)
    upper = jnp.where(iota((CHUNK, CHUNK), 0) <= iota((CHUNK, CHUNK), 1), 1.0, 0.0).astype(BF16)

    chunks = ROWS // CHUNK

    def stack(ref):
        return jnp.concatenate([ref[:, k * CHUNK : (k + 1) * CHUNK] for k in range(chunks)], axis=0)

    log_decay = stack(ld_ref)
    high, low = split2(log_decay)
    rest = ((log_decay - high.astype(F32)) - low.astype(F32)).astype(BF16)
    run = nn(high, upper) + nn(low, upper) + nn(rest, upper)
    middle = jnp.broadcast_to(run[:, CHUNK // 2 - 1 : CHUNK // 2], run.shape)
    total = jnp.broadcast_to(run[:, CHUNK - 1 : CHUNK], run.shape)
    wa_ref[...] = jnp.exp(run - middle)
    wb_ref[...] = jnp.exp(middle - run) * stack(dt_ref)
    column = iota((HEADS, CHUNK), 1)
    logs = jnp.zeros((HEADS, CHUNK), F32)
    before = jnp.zeros((HEADS, CHUNK), F32)
    for k in range(chunks):
        mid_k = middle[k * HEADS : (k + 1) * HEADS]
        tot_k = total[k * HEADS : (k + 1) * HEADS]
        logs = jnp.where(column == k, tot_k - mid_k, logs)
        logs = jnp.where(column == 4 + k, mid_k, logs)
        logs = jnp.where(column == 8 + k, tot_k, logs)
        logs = jnp.where(column == 12 + k, before, logs)
        before = before + tot_k
    logs = jnp.where(column == 16, before, logs)
    sc_ref[...] = per_channel(jnp.exp(logs), expand)[0:32]
    s_ref[...] = jnp.zeros_like(s_ref)

    def local_chunk(k, carry):
        rows = pl.ds(pl.multiple_of(k * CHUNK, CHUNK), CHUNK)
        heads = pl.ds(pl.multiple_of(k * HEADS, HEADS), HEADS)
        factor = per_channel(wb_ref[heads, :], expand)
        u = (x_ref[rows, :].astype(F32) * factor).astype(BF16)
        us_ref[pl.ds(pl.multiple_of(k * 2 * CHUNK, CHUNK), CHUNK), :] = u
        fresh = tn(b_ref[rows, :], u)
        state = s_ref[...]
        sloc_ref[pl.ds(pl.multiple_of(k * STATE, STATE), STATE), :] = state
        s_ref[...] = sc_ref[pl.ds(8 + k, 1), :] * state + sc_ref[pl.ds(k, 1), :] * fresh
        return carry

    lax.fori_loop(0, chunks, local_chunk, 0)

    pl.semaphore_wait(barrier, 7)

    def to_peer(h, slot):
        return pltpu.make_async_remote_copy(
            src_ref=e_send.at[h], dst_ref=e_recv.at[h], send_sem=e_ss.at[slot], recv_sem=e_rs.at[slot],
            device_id={"ctx": peer}, device_id_type=pl.DeviceIdType.MESH,
        )

    e_copies = []
    for slot, (h, lanes) in enumerate([(1 - core, pl.ds(other, HALF)), (core, pl.ds(mine, HALF))]):
        e_send[h, 0:HEAD_ROWS, :] = decay_rows(sc_ref[16:17, lanes])
        e_send[h, HEAD_ROWS:, :] = s_ref[:, lanes].astype(BF16)
        copy = to_peer(h, slot)
        copy.start()
        e_copies.append(copy)

    skip_row = nn(jnp.concatenate(split2(skip_ref[...]), axis=1), expand)

    def gate(k):
        rows = slice(k * CHUNK, (k + 1) * CHUNK)
        after = per_channel(wa_ref[k * HEADS : (k + 1) * HEADS, :], expand)
        v = z_ref[rows, :].astype(F32)
        gated = v / (1.0 + jnp.exp(-v))
        ga_ref[rows, :] = after * gated
        gx_ref[rows, :] = skip_row * x_ref[rows, :].astype(F32) * gated

    to_peer(core, 0).wait_recv()
    is_late = core == 1
    d_mine = sc_ref[16:17, pl.ds(mine, HALF)]
    d_peer = decay_of(e_recv[core, 0:HEAD_ROWS, :])
    block_decay = d_mine * d_peer
    scale_mine = jnp.where(is_late, 1.0, d_peer)
    scale_peer = jnp.where(is_late, d_mine, 1.0)

    def level_copy(l, p):
        rows = slice(0 if p == 0 else HEAD_ROWS + p * PROWS, HEAD_ROWS + (p + 1) * PROWS)
        return pltpu.make_async_remote_copy(
            src_ref=lv_send.at[l, rows, :], dst_ref=lv_recv.at[l, rows, :],
            send_sem=lv_ss.at[l, p], recv_sem=lv_rs.at[l, p],
            device_id={"ctx": partners[l]}, device_id_type=pl.DeviceIdType.MESH,
        )

    def send_level(l, p, state, decay):
        if p == 0:
            lv_send[l, 0:HEAD_ROWS, :] = decay_rows(decay)
        lv_send[l, HEAD_ROWS + p * PROWS : HEAD_ROWS + (p + 1) * PROWS, :] = state.astype(BF16)
        level_copy(l, p).start()

    for p in range(PIECES):
        rows = slice(p * PROWS, (p + 1) * PROWS)
        theirs = e_recv[core, HEAD_ROWS + p * PROWS : HEAD_ROWS + (p + 1) * PROWS, :].astype(F32)
        state = scale_mine * s_ref[rows, pl.ds(mine, HALF)] + scale_peer * theirs
        t_ref[rows, :] = state
        send_level(0, p, state, block_decay)

    def pre_copy(p):
        rows = slice(p * PROWS, (p + 1) * PROWS)
        return pltpu.make_async_remote_copy(
            src_ref=pre_send.at[rows, :], dst_ref=pre_recv.at[rows, :], send_sem=pre_ss.at[p], recv_sem=pre_rs.at[p],
            device_id={"ctx": peer}, device_id_type=pl.DeviceIdType.MESH,
        )

    z_copy.wait()
    prefix_decay = jnp.ones((1, HALF), F32)
    for l in range(LEVELS):
        gate(l)
        up = later[l] == 1
        for p in range(PIECES):
            rows = slice(p * PROWS, (p + 1) * PROWS)
            level_copy(l, p).wait_recv()
            if p == 0:
                their_decay = decay_of(lv_recv[l, 0:HEAD_ROWS, :])
                to_prefix = jnp.where(up, prefix_decay, 0.0)
                scale_theirs = jnp.where(up, block_decay, 1.0)
                scale_ours = jnp.where(up, 1.0, their_decay)
                next_decay = block_decay * their_decay
            theirs = lv_recv[l, HEAD_ROWS + p * PROWS : HEAD_ROWS + (p + 1) * PROWS, :].astype(F32)
            if l < LEVELS - 1:
                state = scale_theirs * theirs + scale_ours * t_ref[rows, :]
                t_ref[rows, :] = state
                send_level(l + 1, p, state, next_decay)
            gain = to_prefix * theirs
            prefix = gain if l == 0 else p_ref[rows, :] + gain
            if l < LEVELS - 1:
                p_ref[rows, :] = prefix
            else:
                pre_send[rows, :] = prefix.astype(BF16)
                pre_copy(p).start()
        prefix_decay = jnp.where(up, prefix_decay * their_decay, prefix_decay)
        block_decay = next_decay

    to_peer(1 - core, 1).wait_recv()

    def finish(p, h, lanes, ref):
        piece = slice(p * PROWS, (p + 1) * PROWS)
        theirs = e_recv[h, HEAD_ROWS + p * PROWS : HEAD_ROWS + (p + 1) * PROWS, :].astype(F32)
        decay = decay_of(e_recv[h, 0:HEAD_ROWS, :])
        start = jnp.where(is_late, decay, 1.0) * ref[piece, :].astype(F32) + jnp.where(is_late, theirs, 0.0)
        for k in range(chunks):
            kept = slice(k * STATE + p * PROWS, k * STATE + (p + 1) * PROWS)
            state = sloc_ref[kept, lanes] + sc_ref[12 + k : 13 + k, lanes] * start
            rows = slice((2 * k + 1) * CHUNK + p * PROWS, (2 * k + 1) * CHUNK + (p + 1) * PROWS)
            us_ref[rows, lanes] = (sc_ref[4 + k : 5 + k, lanes] * state).astype(BF16)

    for p in range(PIECES):
        finish(p, core, pl.ds(mine, HALF), pre_send)
    for p in range(PIECES):
        pre_copy(p).wait_recv()
        finish(p, 1 - core, pl.ds(other, HALF), pre_recv)

    def norm_block(i, carry):
        away = lax.div(i, 2) + 1
        step = jnp.where(i == TP - 1, 0, away * (2 * lax.rem(i, 2) - 1))
        block = lax.rem(z + step + TP, TP)
        k = lax.div(block, 2)
        rows = pl.ds(pl.multiple_of(block * BLOCK, BLOCK), BLOCK)
        c = c_ref[rows, :]
        scores = nt(c, b_ref[pl.ds(pl.multiple_of(k * CHUNK, CHUNK), CHUNK), :])
        t = lax.rem(block, 2) * BLOCK + iota((BLOCK, CHUNK), 0)
        scores = jnp.where(t >= iota((BLOCK, CHUNK), 1), scores, 0.0).astype(BF16)
        ssm = nn(jnp.concatenate([scores, c], axis=1), us_ref[pl.ds(pl.multiple_of(k * 2 * CHUNK, CHUNK), 2 * CHUNK), :])
        mixed = ssm * ga_ref[rows, :] + gx_ref[rows, :]
        meansq = jnp.sum(mixed * mixed, axis=1, keepdims=True) * (1.0 / CHAN)
        n_ref[rows, :] = (mixed * lax.rsqrt(meansq + 1e-05) * gain_ref[...]).astype(BF16)
        return carry

    def block_of(d, step):
        return lax.rem(z + (1 + step if d else 2 * TP - 1 - step), TP)

    def project(q, d, start, width):
        pair = jnp.concatenate(
            [n_ref[pl.ds(pl.multiple_of(block_of(d, s) * BLOCK, BLOCK), BLOCK), :] for s in (2 * q, 2 * q + 1)],
            axis=0,
        )
        here = pl.ds(pl.multiple_of(start, width), width)
        there = pl.ds(pl.multiple_of(d * SIDE + start, width), width)
        pr_ref[q % 2, d, :, here] = nn(pair, w_ref[:, there])

    def ring_copy(s, d, j):
        return pltpu.make_async_remote_copy(
            src_ref=rs_send.at[s, d, j], dst_ref=rs_recv.at[s, d, j],
            send_sem=rs_ss.at[s, d, j], recv_sem=rs_rs.at[s, d, j],
            device_id={"tp": ring[d]}, device_id_type=pl.DeviceIdType.MESH,
        )

    def ring_piece(s, d, j):
        rows = slice((s % 2) * BLOCK, (s % 2 + 1) * BLOCK)
        value = pr_ref[(s // 2) % 2, d, rows, pl.ds(pl.multiple_of(j * SUBW, SUBW), SUBW)]
        if s > 0:
            ring_copy(s - 1, d, j).wait_recv()
            value = value + rs_recv[s - 1, d, j].astype(F32)
        if s < TP - 1:
            rs_send[s, d, j] = value.astype(BF16)
            ring_copy(s, d, j).start()
        else:
            o_ref[:, pl.ds(pl.multiple_of(d * SIDE + j * SUBW, SUBW), SUBW)] = value.astype(BF16)

    def ring_step(s):
        def pieces(j, carry):
            for d in range(2):
                if s == 0:
                    project(0, d, j * SUBW, SUBW)
                ring_piece(s, d, j)
                if s == 1:
                    project(1, d, j * SUBW, SUBW)
                elif 2 <= s < TP - 2:
                    project(s // 2 + 1, s % 2, (2 * j + d) * (SUBW // 2), SUBW // 2)
            return carry

        lax.fori_loop(0, SUB, pieces, 0)

    lax.fori_loop(0, 4, norm_block, 0)
    w_copy.wait()
    ring_step(0)
    lax.fori_loop(4, TP, norm_block, 0)
    for s in range(1, TP):
        ring_step(s)

    for copy in e_copies:
        copy.wait_send()
    for p in range(PIECES):
        pre_copy(p).wait_send()
    for l in range(LEVELS):
        for p in range(PIECES):
            level_copy(l, p).wait_send()
    for s in range(TP - 1):
        for d in range(2):
            for j in range(SUB):
                ring_copy(s, d, j).wait_send()


def on_device(x_in, gate_z, b_in, c_in, step_size, log_decay, skip, norm_gain, out_weight):
    vmem = pl.BlockSpec(memory_space=pltpu.VMEM)
    anywhere = pl.BlockSpec(memory_space=pl.ANY)
    dma = pltpu.SemaphoreType.DMA
    return pl.pallas_call(
        kernel,
        out_shape=jax.ShapeDtypeStruct((BLOCK, DOUT), BF16),
        in_specs=[vmem] * 6 + [anywhere, vmem, anywhere],
        out_specs=vmem,
        scratch_shapes=[
            pltpu.VMEM((ROWS, CHAN), BF16),
            pltpu.VMEM((CHAN, DOUT), BF16),
            pltpu.VMEM((64, CHUNK), F32),
            pltpu.VMEM((64, CHUNK), F32),
            pltpu.VMEM((32, CHAN), F32),
            pltpu.VMEM((2 * ROWS, CHAN), BF16),
            pltpu.VMEM((STATE, CHAN), F32),
            pltpu.VMEM((4 * STATE, CHAN), F32),
            pltpu.VMEM((ROWS, CHAN), F32),
            pltpu.VMEM((ROWS, CHAN), F32),
            pltpu.VMEM((2, HEAD_ROWS + STATE, HALF), BF16),
            pltpu.VMEM((2, HEAD_ROWS + STATE, HALF), BF16),
            pltpu.VMEM((LEVELS, HEAD_ROWS + STATE, HALF), BF16),
            pltpu.VMEM((LEVELS, HEAD_ROWS + STATE, HALF), BF16),
            pltpu.VMEM((STATE, HALF), F32),
            pltpu.VMEM((STATE, HALF), F32),
            pltpu.VMEM((STATE, HALF), BF16),
            pltpu.VMEM((STATE, HALF), BF16),
            pltpu.VMEM((ROWS, CHAN), BF16),
            pltpu.VMEM((2, 2, 2 * BLOCK, SIDE), F32),
            pltpu.VMEM((TP - 1, 2, SUB, BLOCK, SUBW), BF16),
            pltpu.VMEM((TP - 1, 2, SUB, BLOCK, SUBW), BF16),
            dma, dma,
            dma((2,)), dma((2,)),
            dma((LEVELS, PIECES)), dma((LEVELS, PIECES)),
            dma((PIECES,)), dma((PIECES,)),
            dma((TP - 1, 2, SUB)), dma((TP - 1, 2, SUB)),
        ],
        compiler_params=pltpu.CompilerParams(
            collective_id=0, has_side_effects=True, vmem_limit_bytes=56 * 1024 * 1024
        ),
        name="state_space_layer",
    )(
        x_in, b_in, step_size.T, log_decay.T, skip.reshape(1, HEADS), norm_gain.reshape(1, CHAN), gate_z, c_in, out_weight,
    )


def solution(mesh):
    placed = (
        P("ctx", "tp"),
        P("ctx", "tp"),
        P("ctx", "tp"),
        P("ctx", "tp"),
        P("ctx", "tp"),
        P("ctx", "tp"),
        P("tp"),
        P("tp"),
        P("tp", None),
    )
    return jax.shard_map(
        on_device, mesh=mesh, in_specs=placed, out_specs=P(("ctx", "tp"), None), check_vma=False
    )
```

```python
import jax
import jax.numpy as jnp
from jax import lax
from jax.experimental import pallas as pl
from jax.experimental.pallas import tpu as pltpu
from jax.sharding import PartitionSpec as P

F32 = jnp.float32
BF16 = jnp.bfloat16
HEADS = 16
HEAD_DIM = 64
STATE = 128
CHUNK = 128
ROWS = 512
CHAN = 1024
HALF = CHAN // 2
DOUT = 4096
TP = 8
BLOCK = ROWS // TP
SIDE = DOUT // 2
SUB = 4
SUBW = SIDE // SUB
LEVELS = 4
PIECES = 8
PROWS = STATE // PIECES
HEAD_ROWS = 16


def iota(shape, dim):
    return lax.broadcasted_iota(jnp.int32, shape, dim)


def split2(v):
    high = v.astype(BF16)
    return high, (v - high.astype(F32)).astype(BF16)


def nn(a, b):
    return lax.dot_general(a, b, (((1,), (0,)), ((), ())), preferred_element_type=F32)


def nt(a, b):
    return lax.dot_general(a, b, (((1,), (1,)), ((), ())), preferred_element_type=F32)


def tn(a, b):
    return lax.dot_general(a, b, (((0,), (0,)), ((), ())), preferred_element_type=F32)


def per_channel(by_head, expand):
    return tn(jnp.concatenate(split2(by_head), axis=0), expand)


def decay_rows(row):
    high, low = split2(row)
    shape = (HEAD_ROWS // 2, row.shape[1])
    both = [jnp.broadcast_to(v.astype(F32), shape) for v in (high, low)]
    return jnp.concatenate(both, axis=0).astype(BF16)


def decay_of(tile):
    tile = tile.astype(F32)
    return tile[0:1] + tile[HEAD_ROWS // 2 : HEAD_ROWS // 2 + 1]


def kernel(
    x_hbm, b_ref, dt_ref, ld_ref, skip_ref, gain_ref, z_hbm, c_hbm, w_hbm,
    o_hbm,
    x_ref, c_ref, o_ref, z_ref, w_ref, wa_ref, wb_ref, sc_ref, us_ref, s_ref, sloc_ref, ga_ref, gx_ref,
    e_send, e_recv, lv_send, lv_recv, t_ref, p_ref, pre_send, pre_recv,
    start_ref, n_ref, pr_ref, rs_send, rs_recv,
    x_sem, c_sem, o_sem, z_sem, w_sem, e_ss, e_rs, lv_ss, lv_rs, pre_ss, pre_rs, rs_ss, rs_rs,
):
    ctx = lax.axis_index("ctx")
    z = lax.axis_index("tp")
    core = lax.rem(ctx, 2)
    y = lax.rem(lax.div(ctx, 2), 4)
    x = lax.div(ctx, 8)
    peer = ctx + 1 - 2 * core
    partners = [
        ctx + 2 * (1 - 2 * lax.rem(y, 2)),
        ctx + 2 * (3 - 2 * y),
        ctx + 8 * (1 - 2 * lax.rem(x, 2)),
        ctx + 8 * (3 - 2 * x),
    ]
    later = [lax.rem(y, 2), lax.div(y, 2), lax.rem(x, 2), lax.div(x, 2)]
    ring = [lax.rem(z + 1, TP), lax.rem(z + TP - 1, TP)]
    mine = pl.multiple_of(core * HALF, HALF)
    other = pl.multiple_of((1 - core) * HALF, HALF)

    barrier = pltpu.get_barrier_semaphore()
    for c in [peer] + partners:
        pl.semaphore_signal(barrier, inc=1, device_id={"ctx": c}, device_id_type=pl.DeviceIdType.MESH)
    for t in ring:
        pl.semaphore_signal(barrier, inc=1, device_id={"tp": t}, device_id_type=pl.DeviceIdType.MESH)

    chunks = ROWS // CHUNK
    x_copies = []
    for k in range(chunks):
        rows = pl.ds(k * CHUNK, CHUNK)
        copy = pltpu.make_async_copy(x_hbm.at[rows, :], x_ref.at[rows, :], x_sem.at[k])
        copy.start()
        x_copies.append(copy)
    z_copy = pltpu.make_async_copy(z_hbm, z_ref, z_sem)
    z_copy.start()
    c_copy = pltpu.make_async_copy(c_hbm, c_ref, c_sem)
    c_copy.start()
    w_copy = pltpu.make_async_copy(w_hbm, w_ref, w_sem)

    lane = iota((HEADS, CHAN), 1)
    first = iota((HEADS, CHAN), 0) * HEAD_DIM
    one_head = jnp.where((lane >= first) & (lane < first + HEAD_DIM), 1.0, 0.0).astype(BF16)
    expand = jnp.concatenate([one_head, one_head], axis=0)
    upper = jnp.where(iota((CHUNK, CHUNK), 0) <= iota((CHUNK, CHUNK), 1), 1.0, 0.0).astype(BF16)

    def stack(ref):
        return jnp.concatenate([ref[:, k * CHUNK : (k + 1) * CHUNK] for k in range(chunks)], axis=0)

    log_decay = stack(ld_ref)
    high, low = split2(log_decay)
    rest = ((log_decay - high.astype(F32)) - low.astype(F32)).astype(BF16)
    run = nn(high, upper) + nn(low, upper) + nn(rest, upper)
    middle = jnp.broadcast_to(run[:, CHUNK // 2 - 1 : CHUNK // 2], run.shape)
    total = jnp.broadcast_to(run[:, CHUNK - 1 : CHUNK], run.shape)
    wa_ref[...] = jnp.exp(run - middle)
    wb_ref[...] = jnp.exp(middle - run) * stack(dt_ref)
    column = iota((HEADS, CHUNK), 1)
    logs = jnp.zeros((HEADS, CHUNK), F32)
    before = jnp.zeros((HEADS, CHUNK), F32)
    for k in range(chunks):
        mid_k = middle[k * HEADS : (k + 1) * HEADS]
        tot_k = total[k * HEADS : (k + 1) * HEADS]
        logs = jnp.where(column == k, tot_k - mid_k, logs)
        logs = jnp.where(column == 4 + k, mid_k, logs)
        logs = jnp.where(column == 8 + k, tot_k, logs)
        logs = jnp.where(column == 12 + k, before, logs)
        before = before + tot_k
    logs = jnp.where(column == 16, before, logs)
    sc_ref[...] = per_channel(jnp.exp(logs), expand)[0:32]
    for k in range(chunks):
        rows = slice(k * CHUNK, (k + 1) * CHUNK)
        factor = per_channel(wb_ref[k * HEADS : (k + 1) * HEADS, :], expand)
        x_copies[k].wait()
        u = (x_ref[rows, :].astype(F32) * factor).astype(BF16)
        us_ref[2 * k * CHUNK : (2 * k + 1) * CHUNK, :] = u
        fresh = sc_ref[k : k + 1, :] * tn(b_ref[rows, :], u)
        if k == 0:
            s_ref[...] = fresh
        else:
            state = s_ref[...]
            sloc_ref[k * STATE : (k + 1) * STATE, :] = state
            s_ref[...] = sc_ref[8 + k : 9 + k, :] * state + fresh
    sloc_ref[0:STATE, :] = jnp.zeros((STATE, CHAN), F32)
    w_copy.start()

    pl.semaphore_wait(barrier, 7)

    def to_peer(h, slot):
        return pltpu.make_async_remote_copy(
            src_ref=e_send.at[h], dst_ref=e_recv.at[h], send_sem=e_ss.at[slot], recv_sem=e_rs.at[slot],
            device_id={"ctx": peer}, device_id_type=pl.DeviceIdType.MESH,
        )

    e_copies = []
    for slot, (h, lanes) in enumerate([(1 - core, pl.ds(other, HALF)), (core, pl.ds(mine, HALF))]):
        e_send[h, 0:HEAD_ROWS, :] = decay_rows(sc_ref[16:17, lanes])
        e_send[h, HEAD_ROWS:, :] = s_ref[:, lanes].astype(BF16)
        copy = to_peer(h, slot)
        copy.start()
        e_copies.append(copy)

    skip_row = nn(jnp.concatenate(split2(skip_ref[...]), axis=1), expand)

    def gate(k):
        rows = slice(k * CHUNK, (k + 1) * CHUNK)
        after = per_channel(wa_ref[k * HEADS : (k + 1) * HEADS, :], expand)
        v = z_ref[rows, :].astype(F32)
        gated = v / (1.0 + jnp.exp(-v))
        ga_ref[rows, :] = after * gated
        gx_ref[rows, :] = skip_row * x_ref[rows, :].astype(F32) * gated

    to_peer(core, 0).wait_recv()
    is_late = core == 1
    d_mine = sc_ref[16:17, pl.ds(mine, HALF)]
    d_peer = decay_of(e_recv[core, 0:HEAD_ROWS, :])
    block_decay = d_mine * d_peer
    scale_mine = jnp.where(is_late, 1.0, d_peer)
    scale_peer = jnp.where(is_late, d_mine, 1.0)

    def level_copy(l, p):
        rows = slice(0 if p == 0 else HEAD_ROWS + p * PROWS, HEAD_ROWS + (p + 1) * PROWS)
        return pltpu.make_async_remote_copy(
            src_ref=lv_send.at[l, rows, :], dst_ref=lv_recv.at[l, rows, :],
            send_sem=lv_ss.at[l, p], recv_sem=lv_rs.at[l, p],
            device_id={"ctx": partners[l]}, device_id_type=pl.DeviceIdType.MESH,
        )

    def send_level(l, p, state, decay):
        if p == 0:
            lv_send[l, 0:HEAD_ROWS, :] = decay_rows(decay)
        lv_send[l, HEAD_ROWS + p * PROWS : HEAD_ROWS + (p + 1) * PROWS, :] = state.astype(BF16)
        level_copy(l, p).start()

    for p in range(PIECES):
        rows = slice(p * PROWS, (p + 1) * PROWS)
        theirs = e_recv[core, HEAD_ROWS + p * PROWS : HEAD_ROWS + (p + 1) * PROWS, :].astype(F32)
        state = scale_mine * s_ref[rows, pl.ds(mine, HALF)] + scale_peer * theirs
        t_ref[rows, :] = state
        send_level(0, p, state, block_decay)

    def pre_copy(p):
        rows = slice(p * PROWS, (p + 1) * PROWS)
        return pltpu.make_async_remote_copy(
            src_ref=pre_send.at[rows, :], dst_ref=pre_recv.at[rows, :], send_sem=pre_ss.at[p], recv_sem=pre_rs.at[p],
            device_id={"ctx": peer}, device_id_type=pl.DeviceIdType.MESH,
        )

    z_copy.wait()
    prefix_decay = jnp.ones((1, HALF), F32)
    for l in range(LEVELS):
        gate(l)
        up = later[l] == 1
        for p in range(PIECES):
            rows = slice(p * PROWS, (p + 1) * PROWS)
            level_copy(l, p).wait_recv()
            if p == 0:
                their_decay = decay_of(lv_recv[l, 0:HEAD_ROWS, :])
                to_prefix = jnp.where(up, prefix_decay, 0.0)
                scale_theirs = jnp.where(up, block_decay, 1.0)
                scale_ours = jnp.where(up, 1.0, their_decay)
                next_decay = block_decay * their_decay
            theirs = lv_recv[l, HEAD_ROWS + p * PROWS : HEAD_ROWS + (p + 1) * PROWS, :].astype(F32)
            if l < LEVELS - 1:
                state = scale_theirs * theirs + scale_ours * t_ref[rows, :]
                t_ref[rows, :] = state
                send_level(l + 1, p, state, next_decay)
            gain = to_prefix * theirs
            prefix = gain if l == 0 else p_ref[rows, :] + gain
            if l < LEVELS - 1:
                p_ref[rows, :] = prefix
            else:
                pre_send[rows, :] = prefix.astype(BF16)
                pre_copy(p).start()
        prefix_decay = jnp.where(up, prefix_decay * their_decay, prefix_decay)
        block_decay = next_decay

    to_peer(1 - core, 1).wait_recv()

    def arrive(p, h, lanes, ref):
        piece = slice(p * PROWS, (p + 1) * PROWS)
        theirs = e_recv[h, HEAD_ROWS + p * PROWS : HEAD_ROWS + (p + 1) * PROWS, :].astype(F32)
        decay = decay_of(e_recv[h, 0:HEAD_ROWS, :])
        start = jnp.where(is_late, decay, 1.0) * ref[piece, :].astype(F32) + jnp.where(is_late, theirs, 0.0)
        start_ref[piece, lanes] = start

    for p in range(PIECES):
        arrive(p, core, pl.ds(mine, HALF), pre_send)
    for p in range(PIECES):
        pre_copy(p).wait_recv()
        arrive(p, 1 - core, pl.ds(other, HALF), pre_recv)

    c_copy.wait()
    first_chunk = lax.div(lax.rem(z + TP - 1, TP), 2)

    def chunk_state(i, carry):
        k = lax.rem(first_chunk + i, chunks)
        state = sloc_ref[pl.ds(pl.multiple_of(k * STATE, STATE), STATE), :] + sc_ref[pl.ds(12 + k, 1), :] * start_ref[...]
        us_ref[pl.ds(pl.multiple_of((2 * k + 1) * CHUNK, CHUNK), CHUNK), :] = (sc_ref[pl.ds(4 + k, 1), :] * state).astype(BF16)
        return carry

    def norm_block(i, carry):
        away = lax.div(i, 2) + 1
        step = jnp.where(i == TP - 1, 0, away * (2 * lax.rem(i, 2) - 1))
        block = lax.rem(z + step + TP, TP)
        k = lax.div(block, 2)
        rows = pl.ds(pl.multiple_of(block * BLOCK, BLOCK), BLOCK)
        c = c_ref[rows, :]
        scores = nt(c, b_ref[pl.ds(pl.multiple_of(k * CHUNK, CHUNK), CHUNK), :])
        t = lax.rem(block, 2) * BLOCK + iota((BLOCK, CHUNK), 0)
        scores = jnp.where(t >= iota((BLOCK, CHUNK), 1), scores, 0.0).astype(BF16)
        ssm = nn(jnp.concatenate([scores, c], axis=1), us_ref[pl.ds(pl.multiple_of(k * 2 * CHUNK, CHUNK), 2 * CHUNK), :])
        mixed = ssm * ga_ref[rows, :] + gx_ref[rows, :]
        meansq = jnp.sum(mixed * mixed, axis=1, keepdims=True) * (1.0 / CHAN)
        n_ref[rows, :] = (mixed * lax.rsqrt(meansq + 1e-05) * gain_ref[...]).astype(BF16)
        return carry

    def block_of(d, step):
        return lax.rem(z + (1 + step if d else 2 * TP - 1 - step), TP)

    def project(unit, d, j):
        steps = [t for t in (2 * unit - 1, 2 * unit) if 0 <= t < TP]
        parts = [n_ref[pl.ds(pl.multiple_of(block_of(d, t) * BLOCK, BLOCK), BLOCK), :] for t in steps]
        rows = parts[0] if len(parts) == 1 else jnp.concatenate(parts, axis=0)
        here = pl.ds(pl.multiple_of(j * SUBW, SUBW), SUBW)
        there = pl.ds(pl.multiple_of(d * SIDE + j * SUBW, SUBW), SUBW)
        pr_ref[unit % 2, d, 0 : len(steps) * BLOCK, here] = nn(rows, w_ref[:, there])

    def ring_copy(s, d, j):
        return pltpu.make_async_remote_copy(
            src_ref=rs_send.at[s, d, j], dst_ref=rs_recv.at[s, d, j],
            send_sem=rs_ss.at[s, d, j], recv_sem=rs_rs.at[s, d, j],
            device_id={"tp": ring[d]}, device_id_type=pl.DeviceIdType.MESH,
        )

    def out_copy(d, j):
        lanes = pl.ds(pl.multiple_of(d * SIDE + j * SUBW, SUBW), SUBW)
        return pltpu.make_async_copy(o_ref.at[:, lanes], o_hbm.at[:, lanes], o_sem.at[d, j])

    def ring_piece(s, d, j):
        unit = (s + 1) // 2
        low = BLOCK if s > 0 and s % 2 == 0 else 0
        value = pr_ref[unit % 2, d, low : low + BLOCK, pl.ds(pl.multiple_of(j * SUBW, SUBW), SUBW)]
        if s > 0:
            ring_copy(s - 1, d, j).wait_recv()
            value = value + rs_recv[s - 1, d, j].astype(F32)
        if s < TP - 1:
            rs_send[s, d, j] = value.astype(BF16)
            ring_copy(s, d, j).start()
        else:
            o_ref[:, pl.ds(pl.multiple_of(d * SIDE + j * SUBW, SUBW), SUBW)] = value.astype(BF16)
            out_copy(d, j).start()

    def ring_step(s):
        def pieces(j, carry):
            for d in range(2):
                if s < 2:
                    project(s, d, j)
                ring_piece(s, d, j)
                if s > 0 and s % 2 == 0:
                    project(s // 2 + 1, d, j)
            return carry

        lax.fori_loop(0, SUB, pieces, 0)

    lax.fori_loop(0, 2, chunk_state, 0)
    lax.fori_loop(0, 2, norm_block, 0)
    w_copy.wait()
    ring_step(0)
    lax.fori_loop(2, chunks, chunk_state, 0)
    lax.fori_loop(2, 6, norm_block, 0)
    ring_step(1)
    lax.fori_loop(6, TP, norm_block, 0)
    for s in range(2, TP):
        ring_step(s)

    for d in range(2):
        for j in range(SUB):
            out_copy(d, j).wait()
    for copy in e_copies:
        copy.wait_send()
    for p in range(PIECES):
        pre_copy(p).wait_send()
    for l in range(LEVELS):
        for p in range(PIECES):
            level_copy(l, p).wait_send()
    for s in range(TP - 1):
        for d in range(2):
            for j in range(SUB):
                ring_copy(s, d, j).wait_send()


def on_device(x_in, gate_z, b_in, c_in, step_size, log_decay, skip, norm_gain, out_weight):
    vmem = pl.BlockSpec(memory_space=pltpu.VMEM)
    anywhere = pl.BlockSpec(memory_space=pl.ANY)
    dma = pltpu.SemaphoreType.DMA
    return pl.pallas_call(
        kernel,
        out_shape=jax.ShapeDtypeStruct((BLOCK, DOUT), BF16),
        in_specs=[anywhere] + [vmem] * 5 + [anywhere] * 3,
        out_specs=anywhere,
        scratch_shapes=[
            pltpu.VMEM((ROWS, CHAN), BF16),
            pltpu.VMEM((ROWS, STATE), BF16),
            pltpu.VMEM((BLOCK, DOUT), BF16),
            pltpu.VMEM((ROWS, CHAN), BF16),
            pltpu.VMEM((CHAN, DOUT), BF16),
            pltpu.VMEM((64, CHUNK), F32),
            pltpu.VMEM((64, CHUNK), F32),
            pltpu.VMEM((32, CHAN), F32),
            pltpu.VMEM((2 * ROWS, CHAN), BF16),
            pltpu.VMEM((STATE, CHAN), F32),
            pltpu.VMEM((4 * STATE, CHAN), F32),
            pltpu.VMEM((ROWS, CHAN), F32),
            pltpu.VMEM((ROWS, CHAN), F32),
            pltpu.VMEM((2, HEAD_ROWS + STATE, HALF), BF16),
            pltpu.VMEM((2, HEAD_ROWS + STATE, HALF), BF16),
            pltpu.VMEM((LEVELS, HEAD_ROWS + STATE, HALF), BF16),
            pltpu.VMEM((LEVELS, HEAD_ROWS + STATE, HALF), BF16),
            pltpu.VMEM((STATE, HALF), F32),
            pltpu.VMEM((STATE, HALF), F32),
            pltpu.VMEM((STATE, HALF), BF16),
            pltpu.VMEM((STATE, HALF), BF16),
            pltpu.VMEM((STATE, CHAN), F32),
            pltpu.VMEM((ROWS, CHAN), BF16),
            pltpu.VMEM((2, 2, 2 * BLOCK, SIDE), F32),
            pltpu.VMEM((TP - 1, 2, SUB, BLOCK, SUBW), BF16),
            pltpu.VMEM((TP - 1, 2, SUB, BLOCK, SUBW), BF16),
            dma((4,)), dma, dma((2, SUB)), dma, dma,
            dma((2,)), dma((2,)),
            dma((LEVELS, PIECES)), dma((LEVELS, PIECES)),
            dma((PIECES,)), dma((PIECES,)),
            dma((TP - 1, 2, SUB)), dma((TP - 1, 2, SUB)),
        ],
        compiler_params=pltpu.CompilerParams(
            collective_id=0, has_side_effects=True, vmem_limit_bytes=56 * 1024 * 1024
        ),
        name="state_space_layer",
    )(
        x_in, b_in, step_size.T, log_decay.T, skip.reshape(1, HEADS), norm_gain.reshape(1, CHAN), gate_z, c_in, out_weight,
    )


def solution(mesh):
    placed = (
        P("ctx", "tp"),
        P("ctx", "tp"),
        P("ctx", "tp"),
        P("ctx", "tp"),
        P("ctx", "tp"),
        P("ctx", "tp"),
        P("tp"),
        P("tp"),
        P("tp", None),
    )
    return jax.shard_map(
        on_device, mesh=mesh, in_specs=placed, out_specs=P(("ctx", "tp"), None), check_vma=False
    )
```

```python
import jax
import jax.numpy as jnp
from jax import lax
from jax.experimental import pallas as pl
from jax.experimental.pallas import tpu as pltpu
from jax.sharding import PartitionSpec as P

F32 = jnp.float32
BF16 = jnp.bfloat16
HEADS = 16
HEAD_DIM = 64
STATE = 128
CHUNK = 128
ROWS = 512
CHAN = 1024
HALF = CHAN // 2
DOUT = 4096
TP = 8
BLOCK = ROWS // TP
SIDE = DOUT // 2
SUB = 4
SUBW = SIDE // SUB
LEVELS = 4
PIECES = 8
PROWS = STATE // PIECES
HEAD_ROWS = 16


def iota(shape, dim):
    return lax.broadcasted_iota(jnp.int32, shape, dim)


def split2(v):
    high = v.astype(BF16)
    return high, (v - high.astype(F32)).astype(BF16)


def nn(a, b):
    return lax.dot_general(a, b, (((1,), (0,)), ((), ())), preferred_element_type=F32)


def nt(a, b):
    return lax.dot_general(a, b, (((1,), (1,)), ((), ())), preferred_element_type=F32)


def tn(a, b):
    return lax.dot_general(a, b, (((0,), (0,)), ((), ())), preferred_element_type=F32)


def per_channel(by_head, expand):
    return tn(jnp.concatenate(split2(by_head), axis=0), expand)


def decay_rows(row):
    high, low = split2(row)
    shape = (HEAD_ROWS // 2, row.shape[1])
    both = [jnp.broadcast_to(v.astype(F32), shape) for v in (high, low)]
    return jnp.concatenate(both, axis=0).astype(BF16)


def decay_of(tile):
    tile = tile.astype(F32)
    return tile[0:1] + tile[HEAD_ROWS // 2 : HEAD_ROWS // 2 + 1]


def kernel(
    x_hbm, b_hbm, dt_hbm, ld_hbm, skip_hbm, gain_hbm, z_hbm, c_hbm, w_hbm,
    o_ref,
    x_ref, b_ref, dt_ref, ld_ref, skip_ref, gain_ref, c_ref, z_ref, w_ref, wa_ref, wb_ref, sc_ref, us_ref, s_ref, sloc_ref, ga_ref, gx_ref,
    e_send, e_recv, lv_send, lv_recv, t_ref, p_ref, pre_send, pre_recv,
    start_ref, n_ref, pr_ref, rs_send, rs_recv,
    x_sem, small_sem, c_sem, z_sem, w_sem, e_ss, e_rs, lv_ss, lv_rs, pre_ss, pre_rs, rs_ss, rs_rs,
):
    ctx = lax.axis_index("ctx")
    z = lax.axis_index("tp")
    core = lax.rem(ctx, 2)
    y = lax.rem(lax.div(ctx, 2), 4)
    x = lax.div(ctx, 8)
    peer = ctx + 1 - 2 * core
    partners = [
        ctx + 2 * (1 - 2 * lax.rem(y, 2)),
        ctx + 2 * (3 - 2 * y),
        ctx + 8 * (1 - 2 * lax.rem(x, 2)),
        ctx + 8 * (3 - 2 * x),
    ]
    later = [lax.rem(y, 2), lax.div(y, 2), lax.rem(x, 2), lax.div(x, 2)]
    ring = [lax.rem(z + 1, TP), lax.rem(z + TP - 1, TP)]
    mine = pl.multiple_of(core * HALF, HALF)
    other = pl.multiple_of((1 - core) * HALF, HALF)

    barrier = pltpu.get_barrier_semaphore()
    for c in [peer] + partners:
        pl.semaphore_signal(barrier, inc=1, device_id={"ctx": c}, device_id_type=pl.DeviceIdType.MESH)
    for t in ring:
        pl.semaphore_signal(barrier, inc=1, device_id={"tp": t}, device_id_type=pl.DeviceIdType.MESH)

    small = [(ld_hbm, ld_ref), (dt_hbm, dt_ref), (b_hbm, b_ref), (skip_hbm, skip_ref), (gain_hbm, gain_ref)]
    small = [pltpu.make_async_copy(a, b, small_sem.at[i]) for i, (a, b) in enumerate(small)]
    for copy in small[:3]:
        copy.start()
    chunks = ROWS // CHUNK
    x_copies = []
    for k in range(chunks):
        rows = pl.ds(k * CHUNK, CHUNK)
        copy = pltpu.make_async_copy(x_hbm.at[rows, :], x_ref.at[rows, :], x_sem.at[k])
        copy.start()
        x_copies.append(copy)
    z_copy = pltpu.make_async_copy(z_hbm, z_ref, z_sem)
    z_copy.start()
    for copy in small[3:]:
        copy.start()
    c_copy = pltpu.make_async_copy(c_hbm, c_ref, c_sem)
    c_copy.start()
    w_copy = pltpu.make_async_copy(w_hbm, w_ref, w_sem)

    lane = iota((HEADS, CHAN), 1)
    first = iota((HEADS, CHAN), 0) * HEAD_DIM
    one_head = jnp.where((lane >= first) & (lane < first + HEAD_DIM), 1.0, 0.0).astype(BF16)
    expand = jnp.concatenate([one_head, one_head], axis=0)
    upper = jnp.where(iota((CHUNK, CHUNK), 0) <= iota((CHUNK, CHUNK), 1), 1.0, 0.0).astype(BF16)

    def stack(ref):
        return jnp.concatenate([ref[:, k * CHUNK : (k + 1) * CHUNK] for k in range(chunks)], axis=0)

    small[0].wait()
    log_decay = stack(ld_ref)
    high, low = split2(log_decay)
    rest = ((log_decay - high.astype(F32)) - low.astype(F32)).astype(BF16)
    run = nn(high, upper) + nn(low, upper) + nn(rest, upper)
    middle = jnp.broadcast_to(run[:, CHUNK // 2 - 1 : CHUNK // 2], run.shape)
    total = jnp.broadcast_to(run[:, CHUNK - 1 : CHUNK], run.shape)
    wa_ref[...] = jnp.exp(run - middle)
    small[1].wait()
    wb_ref[...] = jnp.exp(middle - run) * stack(dt_ref)
    column = iota((HEADS, CHUNK), 1)
    logs = jnp.zeros((HEADS, CHUNK), F32)
    before = jnp.zeros((HEADS, CHUNK), F32)
    for k in range(chunks):
        mid_k = middle[k * HEADS : (k + 1) * HEADS]
        tot_k = total[k * HEADS : (k + 1) * HEADS]
        logs = jnp.where(column == k, tot_k - mid_k, logs)
        logs = jnp.where(column == 4 + k, mid_k, logs)
        logs = jnp.where(column == 8 + k, tot_k, logs)
        logs = jnp.where(column == 12 + k, before, logs)
        before = before + tot_k
    logs = jnp.where(column == 16, before, logs)
    sc_ref[...] = per_channel(jnp.exp(logs), expand)[0:32]
    small[2].wait()
    for k in range(chunks):
        rows = slice(k * CHUNK, (k + 1) * CHUNK)
        factor = per_channel(wb_ref[k * HEADS : (k + 1) * HEADS, :], expand)
        x_copies[k].wait()
        u = (x_ref[rows, :].astype(F32) * factor).astype(BF16)
        us_ref[2 * k * CHUNK : (2 * k + 1) * CHUNK, :] = u
        fresh = sc_ref[k : k + 1, :] * tn(b_ref[rows, :], u)
        if k == 0:
            s_ref[...] = fresh
        else:
            state = s_ref[...]
            sloc_ref[k * STATE : (k + 1) * STATE, :] = state
            s_ref[...] = sc_ref[8 + k : 9 + k, :] * state + fresh
    sloc_ref[0:STATE, :] = jnp.zeros((STATE, CHAN), F32)
    w_copy.start()

    pl.semaphore_wait(barrier, 7)

    def to_peer(h, slot):
        return pltpu.make_async_remote_copy(
            src_ref=e_send.at[h], dst_ref=e_recv.at[h], send_sem=e_ss.at[slot], recv_sem=e_rs.at[slot],
            device_id={"ctx": peer}, device_id_type=pl.DeviceIdType.MESH,
        )

    e_copies = []
    for slot, (h, lanes) in enumerate([(1 - core, pl.ds(other, HALF)), (core, pl.ds(mine, HALF))]):
        e_send[h, 0:HEAD_ROWS, :] = decay_rows(sc_ref[16:17, lanes])
        e_send[h, HEAD_ROWS:, :] = s_ref[:, lanes].astype(BF16)
        copy = to_peer(h, slot)
        copy.start()
        e_copies.append(copy)

    for copy in small[3:]:
        copy.wait()
    skip_row = nn(jnp.concatenate(split2(skip_ref[...]), axis=1), expand)

    def gate(k):
        rows = slice(k * CHUNK, (k + 1) * CHUNK)
        after = per_channel(wa_ref[k * HEADS : (k + 1) * HEADS, :], expand)
        v = z_ref[rows, :].astype(F32)
        gated = v / (1.0 + jnp.exp(-v))
        ga_ref[rows, :] = after * gated
        gx_ref[rows, :] = skip_row * x_ref[rows, :].astype(F32) * gated

    to_peer(core, 0).wait_recv()
    is_late = core == 1
    d_mine = sc_ref[16:17, pl.ds(mine, HALF)]
    d_peer = decay_of(e_recv[core, 0:HEAD_ROWS, :])
    block_decay = d_mine * d_peer
    scale_mine = jnp.where(is_late, 1.0, d_peer)
    scale_peer = jnp.where(is_late, d_mine, 1.0)

    def level_copy(l, p):
        rows = slice(0 if p == 0 else HEAD_ROWS + p * PROWS, HEAD_ROWS + (p + 1) * PROWS)
        return pltpu.make_async_remote_copy(
            src_ref=lv_send.at[l, rows, :], dst_ref=lv_recv.at[l, rows, :],
            send_sem=lv_ss.at[l, p], recv_sem=lv_rs.at[l, p],
            device_id={"ctx": partners[l]}, device_id_type=pl.DeviceIdType.MESH,
        )

    def send_level(l, p, state, decay):
        if p == 0:
            lv_send[l, 0:HEAD_ROWS, :] = decay_rows(decay)
        lv_send[l, HEAD_ROWS + p * PROWS : HEAD_ROWS + (p + 1) * PROWS, :] = state.astype(BF16)
        level_copy(l, p).start()

    for p in range(PIECES):
        rows = slice(p * PROWS, (p + 1) * PROWS)
        theirs = e_recv[core, HEAD_ROWS + p * PROWS : HEAD_ROWS + (p + 1) * PROWS, :].astype(F32)
        state = scale_mine * s_ref[rows, pl.ds(mine, HALF)] + scale_peer * theirs
        t_ref[rows, :] = state
        send_level(0, p, state, block_decay)

    def pre_copy(p):
        rows = slice(p * PROWS, (p + 1) * PROWS)
        return pltpu.make_async_remote_copy(
            src_ref=pre_send.at[rows, :], dst_ref=pre_recv.at[rows, :], send_sem=pre_ss.at[p], recv_sem=pre_rs.at[p],
            device_id={"ctx": peer}, device_id_type=pl.DeviceIdType.MESH,
        )

    z_copy.wait()
    prefix_decay = jnp.ones((1, HALF), F32)
    for l in range(LEVELS):
        gate(l)
        up = later[l] == 1
        for p in range(PIECES):
            rows = slice(p * PROWS, (p + 1) * PROWS)
            level_copy(l, p).wait_recv()
            if p == 0:
                their_decay = decay_of(lv_recv[l, 0:HEAD_ROWS, :])
                to_prefix = jnp.where(up, prefix_decay, 0.0)
                scale_theirs = jnp.where(up, block_decay, 1.0)
                scale_ours = jnp.where(up, 1.0, their_decay)
                next_decay = block_decay * their_decay
            theirs = lv_recv[l, HEAD_ROWS + p * PROWS : HEAD_ROWS + (p + 1) * PROWS, :].astype(F32)
            if l < LEVELS - 1:
                state = scale_theirs * theirs + scale_ours * t_ref[rows, :]
                t_ref[rows, :] = state
                send_level(l + 1, p, state, next_decay)
            gain = to_prefix * theirs
            prefix = gain if l == 0 else p_ref[rows, :] + gain
            if l < LEVELS - 1:
                p_ref[rows, :] = prefix
            else:
                pre_send[rows, :] = prefix.astype(BF16)
                pre_copy(p).start()
        prefix_decay = jnp.where(up, prefix_decay * their_decay, prefix_decay)
        block_decay = next_decay

    to_peer(1 - core, 1).wait_recv()

    def arrive(p, h, lanes, ref):
        piece = slice(p * PROWS, (p + 1) * PROWS)
        theirs = e_recv[h, HEAD_ROWS + p * PROWS : HEAD_ROWS + (p + 1) * PROWS, :].astype(F32)
        decay = decay_of(e_recv[h, 0:HEAD_ROWS, :])
        start = jnp.where(is_late, decay, 1.0) * ref[piece, :].astype(F32) + jnp.where(is_late, theirs, 0.0)
        start_ref[piece, lanes] = start

    for p in range(PIECES):
        arrive(p, core, pl.ds(mine, HALF), pre_send)
    for p in range(PIECES):
        pre_copy(p).wait_recv()
        arrive(p, 1 - core, pl.ds(other, HALF), pre_recv)

    c_copy.wait()
    first_chunk = lax.div(lax.rem(z + TP - 1, TP), 2)

    def chunk_state(i, carry):
        k = lax.rem(first_chunk + i, chunks)
        state = sloc_ref[pl.ds(pl.multiple_of(k * STATE, STATE), STATE), :] + sc_ref[pl.ds(12 + k, 1), :] * start_ref[...]
        us_ref[pl.ds(pl.multiple_of((2 * k + 1) * CHUNK, CHUNK), CHUNK), :] = (sc_ref[pl.ds(4 + k, 1), :] * state).astype(BF16)
        return carry

    def norm_block(i, carry):
        away = lax.div(i, 2) + 1
        step = jnp.where(i == TP - 1, 0, away * (2 * lax.rem(i, 2) - 1))
        block = lax.rem(z + step + TP, TP)
        k = lax.div(block, 2)
        rows = pl.ds(pl.multiple_of(block * BLOCK, BLOCK), BLOCK)
        c = c_ref[rows, :]
        scores = nt(c, b_ref[pl.ds(pl.multiple_of(k * CHUNK, CHUNK), CHUNK), :])
        t = lax.rem(block, 2) * BLOCK + iota((BLOCK, CHUNK), 0)
        scores = jnp.where(t >= iota((BLOCK, CHUNK), 1), scores, 0.0).astype(BF16)
        ssm = nn(jnp.concatenate([scores, c], axis=1), us_ref[pl.ds(pl.multiple_of(k * 2 * CHUNK, CHUNK), 2 * CHUNK), :])
        mixed = ssm * ga_ref[rows, :] + gx_ref[rows, :]
        meansq = jnp.sum(mixed * mixed, axis=1, keepdims=True) * (1.0 / CHAN)
        n_ref[rows, :] = (mixed * lax.rsqrt(meansq + 1e-05) * gain_ref[...]).astype(BF16)
        return carry

    def block_of(d, step):
        return lax.rem(z + (1 + step if d else 2 * TP - 1 - step), TP)

    def project(unit, d, j):
        steps = [t for t in (2 * unit - 1, 2 * unit) if 0 <= t < TP]
        parts = [n_ref[pl.ds(pl.multiple_of(block_of(d, t) * BLOCK, BLOCK), BLOCK), :] for t in steps]
        rows = parts[0] if len(parts) == 1 else jnp.concatenate(parts, axis=0)
        here = pl.ds(pl.multiple_of(j * SUBW, SUBW), SUBW)
        there = pl.ds(pl.multiple_of(d * SIDE + j * SUBW, SUBW), SUBW)
        pr_ref[unit % 2, d, 0 : len(steps) * BLOCK, here] = nn(rows, w_ref[:, there])

    def ring_copy(s, d, j):
        return pltpu.make_async_remote_copy(
            src_ref=rs_send.at[s, d, j], dst_ref=rs_recv.at[s, d, j],
            send_sem=rs_ss.at[s, d, j], recv_sem=rs_rs.at[s, d, j],
            device_id={"tp": ring[d]}, device_id_type=pl.DeviceIdType.MESH,
        )

    def ring_piece(s, d, j):
        unit = (s + 1) // 2
        low = BLOCK if s > 0 and s % 2 == 0 else 0
        value = pr_ref[unit % 2, d, low : low + BLOCK, pl.ds(pl.multiple_of(j * SUBW, SUBW), SUBW)]
        if s > 0:
            ring_copy(s - 1, d, j).wait_recv()
            value = value + rs_recv[s - 1, d, j].astype(F32)
        if s < TP - 1:
            rs_send[s, d, j] = value.astype(BF16)
            ring_copy(s, d, j).start()
        else:
            o_ref[:, pl.ds(pl.multiple_of(d * SIDE + j * SUBW, SUBW), SUBW)] = value.astype(BF16)

    def ring_step(s):
        def pieces(j, carry):
            for d in range(2):
                if s < 2:
                    project(s, d, j)
                ring_piece(s, d, j)
                if s > 0 and s % 2 == 0:
                    project(s // 2 + 1, d, j)
            return carry

        lax.fori_loop(0, SUB, pieces, 0)

    lax.fori_loop(0, 2, chunk_state, 0)
    lax.fori_loop(0, 2, norm_block, 0)
    w_copy.wait()
    ring_step(0)
    lax.fori_loop(2, chunks, chunk_state, 0)
    lax.fori_loop(2, 6, norm_block, 0)
    ring_step(1)
    lax.fori_loop(6, TP, norm_block, 0)
    for s in range(2, TP):
        ring_step(s)

    for copy in e_copies:
        copy.wait_send()
    for p in range(PIECES):
        pre_copy(p).wait_send()
    for l in range(LEVELS):
        for p in range(PIECES):
            level_copy(l, p).wait_send()
    for s in range(TP - 1):
        for d in range(2):
            for j in range(SUB):
                ring_copy(s, d, j).wait_send()


def on_device(x_in, gate_z, b_in, c_in, step_size, log_decay, skip, norm_gain, out_weight):
    vmem = pl.BlockSpec(memory_space=pltpu.VMEM)
    hbm = pl.BlockSpec(memory_space=pltpu.HBM)
    dma = pltpu.SemaphoreType.DMA
    return pl.pallas_call(
        kernel,
        out_shape=jax.ShapeDtypeStruct((BLOCK, DOUT), BF16),
        in_specs=[hbm] * 9,
        out_specs=vmem,
        scratch_shapes=[
            pltpu.VMEM((ROWS, CHAN), BF16),
            pltpu.VMEM((ROWS, STATE), BF16),
            pltpu.VMEM((HEADS, ROWS), F32),
            pltpu.VMEM((HEADS, ROWS), F32),
            pltpu.VMEM((1, HEADS), F32),
            pltpu.VMEM((1, CHAN), F32),
            pltpu.VMEM((ROWS, STATE), BF16),
            pltpu.VMEM((ROWS, CHAN), BF16),
            pltpu.VMEM((CHAN, DOUT), BF16),
            pltpu.VMEM((64, CHUNK), F32),
            pltpu.VMEM((64, CHUNK), F32),
            pltpu.VMEM((32, CHAN), F32),
            pltpu.VMEM((2 * ROWS, CHAN), BF16),
            pltpu.VMEM((STATE, CHAN), F32),
            pltpu.VMEM((4 * STATE, CHAN), F32),
            pltpu.VMEM((ROWS, CHAN), F32),
            pltpu.VMEM((ROWS, CHAN), F32),
            pltpu.VMEM((2, HEAD_ROWS + STATE, HALF), BF16),
            pltpu.VMEM((2, HEAD_ROWS + STATE, HALF), BF16),
            pltpu.VMEM((LEVELS, HEAD_ROWS + STATE, HALF), BF16),
            pltpu.VMEM((LEVELS, HEAD_ROWS + STATE, HALF), BF16),
            pltpu.VMEM((STATE, HALF), F32),
            pltpu.VMEM((STATE, HALF), F32),
            pltpu.VMEM((STATE, HALF), BF16),
            pltpu.VMEM((STATE, HALF), BF16),
            pltpu.VMEM((STATE, CHAN), F32),
            pltpu.VMEM((ROWS, CHAN), BF16),
            pltpu.VMEM((2, 2, 2 * BLOCK, SIDE), F32),
            pltpu.VMEM((TP - 1, 2, SUB, BLOCK, SUBW), BF16),
            pltpu.VMEM((TP - 1, 2, SUB, BLOCK, SUBW), BF16),
            dma((4,)), dma((5,)), dma, dma, dma,
            dma((2,)), dma((2,)),
            dma((LEVELS, PIECES)), dma((LEVELS, PIECES)),
            dma((PIECES,)), dma((PIECES,)),
            dma((TP - 1, 2, SUB)), dma((TP - 1, 2, SUB)),
        ],
        compiler_params=pltpu.CompilerParams(
            collective_id=0, has_side_effects=True, vmem_limit_bytes=44 * 1024 * 1024
        ),
        name="state_space_layer",
    )(
        *[
            pltpu.with_memory_space_constraint(a, pltpu.HBM)
            for a in (
                x_in, b_in, step_size.T, log_decay.T, skip.reshape(1, HEADS), norm_gain.reshape(1, CHAN),
                gate_z, c_in, out_weight,
            )
        ]
    )


def solution(mesh):
    placed = (
        P("ctx", "tp"),
        P("ctx", "tp"),
        P("ctx", "tp"),
        P("ctx", "tp"),
        P("ctx", "tp"),
        P("ctx", "tp"),
        P("tp"),
        P("tp"),
        P("tp", None),
    )
    return jax.shard_map(
        on_device, mesh=mesh, in_specs=placed, out_specs=P(("ctx", "tp"), None), check_vma=False
    )
```

```python
import jax
import jax.numpy as jnp
from jax import lax
from jax.experimental import pallas as pl
from jax.experimental.pallas import tpu as pltpu
from jax.sharding import PartitionSpec as P

F32 = jnp.float32
BF16 = jnp.bfloat16
HEADS = 16
HEAD_DIM = 64
STATE = 128
CHUNK = 128
ROWS = 512
CHAN = 1024
HALF = CHAN // 2
DOUT = 4096
TP = 8
BLOCK = ROWS // TP
SIDE = DOUT // 2
SUB = 2
SUBW = SIDE // SUB
LEVELS = 4
PIECES = 8
PROWS = STATE // PIECES
HEAD_ROWS = 16


def iota(shape, dim):
    return lax.broadcasted_iota(jnp.int32, shape, dim)


def split2(v):
    high = v.astype(BF16)
    return high, (v - high.astype(F32)).astype(BF16)


def nn(a, b):
    return lax.dot_general(a, b, (((1,), (0,)), ((), ())), preferred_element_type=F32)


def nt(a, b):
    return lax.dot_general(a, b, (((1,), (1,)), ((), ())), preferred_element_type=F32)


def tn(a, b):
    return lax.dot_general(a, b, (((0,), (0,)), ((), ())), preferred_element_type=F32)


def per_channel(by_head, expand):
    return tn(jnp.concatenate(split2(by_head), axis=0), expand)


def decay_rows(row):
    high, low = split2(row)
    shape = (HEAD_ROWS // 2, row.shape[1])
    both = [jnp.broadcast_to(v.astype(F32), shape) for v in (high, low)]
    return jnp.concatenate(both, axis=0).astype(BF16)


def decay_of(tile):
    tile = tile.astype(F32)
    return tile[0:1] + tile[HEAD_ROWS // 2 : HEAD_ROWS // 2 + 1]


def kernel(
    x_hbm, b_hbm, dt_hbm, ld_hbm, skip_hbm, gain_hbm, z_hbm, c_hbm, w_hbm,
    o_ref,
    x_ref, b_ref, dt_ref, ld_ref, skip_ref, gain_ref, c_ref, z_ref, w_ref, wa_ref, wb_ref, sc_ref, us_ref, s_ref, sloc_ref, ga_ref, gx_ref,
    e_send, e_recv, lv_send, lv_recv, t_ref, p_ref, pre_send, pre_recv,
    start_ref, n_ref, pr_ref, rs_send, rs_recv,
    x_sem, small_sem, c_sem, z_sem, w_sem, e_ss, e_rs, lv_ss, lv_rs, pre_ss, pre_rs, rs_ss, rs_rs,
):
    ctx = lax.axis_index("ctx")
    z = lax.axis_index("tp")
    core = lax.rem(ctx, 2)
    y = lax.rem(lax.div(ctx, 2), 4)
    x = lax.div(ctx, 8)
    peer = ctx + 1 - 2 * core
    partners = [
        ctx + 2 * (1 - 2 * lax.rem(y, 2)),
        ctx + 2 * (3 - 2 * y),
        ctx + 8 * (1 - 2 * lax.rem(x, 2)),
        ctx + 8 * (3 - 2 * x),
    ]
    later = [lax.rem(y, 2), lax.div(y, 2), lax.rem(x, 2), lax.div(x, 2)]
    ring = [lax.rem(z + 1, TP), lax.rem(z + TP - 1, TP)]
    mine = pl.multiple_of(core * HALF, HALF)
    other = pl.multiple_of((1 - core) * HALF, HALF)

    barrier = pltpu.get_barrier_semaphore()
    for c in [peer] + partners:
        pl.semaphore_signal(barrier, inc=1, device_id={"ctx": c}, device_id_type=pl.DeviceIdType.MESH)
    for t in ring:
        pl.semaphore_signal(barrier, inc=1, device_id={"tp": t}, device_id_type=pl.DeviceIdType.MESH)

    small = [(ld_hbm, ld_ref), (dt_hbm, dt_ref), (b_hbm, b_ref), (skip_hbm, skip_ref), (gain_hbm, gain_ref)]
    small = [pltpu.make_async_copy(a, b, small_sem.at[i]) for i, (a, b) in enumerate(small)]
    for copy in small[:3]:
        copy.start()
    chunks = ROWS // CHUNK
    x_copies = []
    for k in range(chunks):
        rows = pl.ds(k * CHUNK, CHUNK)
        copy = pltpu.make_async_copy(x_hbm.at[rows, :], x_ref.at[rows, :], x_sem.at[k])
        copy.start()
        x_copies.append(copy)
    z_copy = pltpu.make_async_copy(z_hbm, z_ref, z_sem)
    z_copy.start()
    for copy in small[3:]:
        copy.start()
    c_copy = pltpu.make_async_copy(c_hbm, c_ref, c_sem)
    c_copy.start()
    w_copy = pltpu.make_async_copy(w_hbm, w_ref, w_sem)

    lane = iota((HEADS, CHAN), 1)
    first = iota((HEADS, CHAN), 0) * HEAD_DIM
    one_head = jnp.where((lane >= first) & (lane < first + HEAD_DIM), 1.0, 0.0).astype(BF16)
    expand = jnp.concatenate([one_head, one_head], axis=0)
    upper = jnp.where(iota((CHUNK, CHUNK), 0) <= iota((CHUNK, CHUNK), 1), 1.0, 0.0).astype(BF16)

    def stack(ref):
        return jnp.concatenate([ref[:, k * CHUNK : (k + 1) * CHUNK] for k in range(chunks)], axis=0)

    small[0].wait()
    log_decay = stack(ld_ref)
    high, low = split2(log_decay)
    rest = ((log_decay - high.astype(F32)) - low.astype(F32)).astype(BF16)
    run = nn(high, upper) + nn(low, upper) + nn(rest, upper)
    middle = jnp.broadcast_to(run[:, CHUNK // 2 - 1 : CHUNK // 2], run.shape)
    total = jnp.broadcast_to(run[:, CHUNK - 1 : CHUNK], run.shape)
    wa_ref[...] = jnp.exp(run - middle)
    small[1].wait()
    wb_ref[...] = jnp.exp(middle - run) * stack(dt_ref)
    column = iota((HEADS, CHUNK), 1)
    logs = jnp.zeros((HEADS, CHUNK), F32)
    before = jnp.zeros((HEADS, CHUNK), F32)
    for k in range(chunks):
        mid_k = middle[k * HEADS : (k + 1) * HEADS]
        tot_k = total[k * HEADS : (k + 1) * HEADS]
        logs = jnp.where(column == k, tot_k - mid_k, logs)
        logs = jnp.where(column == 4 + k, mid_k, logs)
        logs = jnp.where(column == 8 + k, tot_k, logs)
        logs = jnp.where(column == 12 + k, before, logs)
        before = before + tot_k
    logs = jnp.where(column == 16, before, logs)
    sc_ref[...] = per_channel(jnp.exp(logs), expand)[0:32]
    small[2].wait()
    for k in range(chunks):
        rows = slice(k * CHUNK, (k + 1) * CHUNK)
        factor = per_channel(wb_ref[k * HEADS : (k + 1) * HEADS, :], expand)
        x_copies[k].wait()
        u = (x_ref[rows, :].astype(F32) * factor).astype(BF16)
        us_ref[2 * k * CHUNK : (2 * k + 1) * CHUNK, :] = u
        fresh = sc_ref[k : k + 1, :] * tn(b_ref[rows, :], u)
        if k == 0:
            s_ref[...] = fresh
        else:
            state = s_ref[...]
            sloc_ref[k * STATE : (k + 1) * STATE, :] = state
            s_ref[...] = sc_ref[8 + k : 9 + k, :] * state + fresh
    sloc_ref[0:STATE, :] = jnp.zeros((STATE, CHAN), F32)
    w_copy.start()

    pl.semaphore_wait(barrier, 7)

    def to_peer(h, slot):
        return pltpu.make_async_remote_copy(
            src_ref=e_send.at[h], dst_ref=e_recv.at[h], send_sem=e_ss.at[slot], recv_sem=e_rs.at[slot],
            device_id={"ctx": peer}, device_id_type=pl.DeviceIdType.MESH,
        )

    e_copies = []
    for slot, (h, lanes) in enumerate([(1 - core, pl.ds(other, HALF)), (core, pl.ds(mine, HALF))]):
        e_send[h, 0:HEAD_ROWS, :] = decay_rows(sc_ref[16:17, lanes])
        e_send[h, HEAD_ROWS:, :] = s_ref[:, lanes].astype(BF16)
        copy = to_peer(h, slot)
        copy.start()
        e_copies.append(copy)

    for copy in small[3:]:
        copy.wait()
    skip_row = nn(jnp.concatenate(split2(skip_ref[...]), axis=1), expand)

    def gate(k):
        rows = slice(k * CHUNK, (k + 1) * CHUNK)
        after = per_channel(wa_ref[k * HEADS : (k + 1) * HEADS, :], expand)
        v = z_ref[rows, :].astype(F32)
        gated = v / (1.0 + jnp.exp(-v))
        ga_ref[rows, :] = after * gated
        gx_ref[rows, :] = skip_row * x_ref[rows, :].astype(F32) * gated

    to_peer(core, 0).wait_recv()
    is_late = core == 1
    d_mine = sc_ref[16:17, pl.ds(mine, HALF)]
    d_peer = decay_of(e_recv[core, 0:HEAD_ROWS, :])
    block_decay = d_mine * d_peer
    scale_mine = jnp.where(is_late, 1.0, d_peer)
    scale_peer = jnp.where(is_late, d_mine, 1.0)

    def level_copy(l, p):
        rows = slice(0 if p == 0 else HEAD_ROWS + p * PROWS, HEAD_ROWS + (p + 1) * PROWS)
        return pltpu.make_async_remote_copy(
            src_ref=lv_send.at[l, rows, :], dst_ref=lv_recv.at[l, rows, :],
            send_sem=lv_ss.at[l, p], recv_sem=lv_rs.at[l, p],
            device_id={"ctx": partners[l]}, device_id_type=pl.DeviceIdType.MESH,
        )

    def send_level(l, p, state, decay):
        if p == 0:
            lv_send[l, 0:HEAD_ROWS, :] = decay_rows(decay)
        lv_send[l, HEAD_ROWS + p * PROWS : HEAD_ROWS + (p + 1) * PROWS, :] = state.astype(BF16)
        if l < LEVELS - 1:
            level_copy(l, p).start()
        else:

            @pl.when(later[l] == 0)
            def _():
                level_copy(l, p).start()

    for p in range(PIECES):
        rows = slice(p * PROWS, (p + 1) * PROWS)
        theirs = e_recv[core, HEAD_ROWS + p * PROWS : HEAD_ROWS + (p + 1) * PROWS, :].astype(F32)
        state = scale_mine * s_ref[rows, pl.ds(mine, HALF)] + scale_peer * theirs
        t_ref[rows, :] = state
        send_level(0, p, state, block_decay)

    def pre_copy(p):
        rows = slice(p * PROWS, (p + 1) * PROWS)
        return pltpu.make_async_remote_copy(
            src_ref=pre_send.at[rows, :], dst_ref=pre_recv.at[rows, :], send_sem=pre_ss.at[p], recv_sem=pre_rs.at[p],
            device_id={"ctx": peer}, device_id_type=pl.DeviceIdType.MESH,
        )

    z_copy.wait()
    prefix_decay = jnp.ones((1, HALF), F32)
    for l in range(LEVELS - 1):
        gate(l)
        up = later[l] == 1
        for p in range(PIECES):
            rows = slice(p * PROWS, (p + 1) * PROWS)
            level_copy(l, p).wait_recv()
            if p == 0:
                their_decay = decay_of(lv_recv[l, 0:HEAD_ROWS, :])
                to_prefix = jnp.where(up, prefix_decay, 0.0)
                scale_theirs = jnp.where(up, block_decay, 1.0)
                scale_ours = jnp.where(up, 1.0, their_decay)
                next_decay = block_decay * their_decay
            theirs = lv_recv[l, HEAD_ROWS + p * PROWS : HEAD_ROWS + (p + 1) * PROWS, :].astype(F32)
            state = scale_theirs * theirs + scale_ours * t_ref[rows, :]
            t_ref[rows, :] = state
            send_level(l + 1, p, state, next_decay)
            gain = to_prefix * theirs
            p_ref[rows, :] = gain if l == 0 else p_ref[rows, :] + gain
        prefix_decay = jnp.where(up, prefix_decay * their_decay, prefix_decay)
        block_decay = next_decay

    last = LEVELS - 1
    gate(last)
    for p in range(PIECES):
        rows = slice(p * PROWS, (p + 1) * PROWS)

        @pl.when(later[last] == 1)
        def _():
            level_copy(last, p).wait_recv()
            theirs = lv_recv[last, HEAD_ROWS + p * PROWS : HEAD_ROWS + (p + 1) * PROWS, :].astype(F32)
            p_ref[rows, :] = p_ref[rows, :] + prefix_decay * theirs

        pre_send[rows, :] = p_ref[rows, :].astype(BF16)
        pre_copy(p).start()

    to_peer(1 - core, 1).wait_recv()

    def arrive(p, h, lanes, ref):
        piece = slice(p * PROWS, (p + 1) * PROWS)
        theirs = e_recv[h, HEAD_ROWS + p * PROWS : HEAD_ROWS + (p + 1) * PROWS, :].astype(F32)
        decay = decay_of(e_recv[h, 0:HEAD_ROWS, :])
        start = jnp.where(is_late, decay, 1.0) * ref[piece, :].astype(F32) + jnp.where(is_late, theirs, 0.0)
        start_ref[piece, lanes] = start

    for p in range(PIECES):
        arrive(p, core, pl.ds(mine, HALF), pre_send)
    for p in range(PIECES):
        pre_copy(p).wait_recv()
        arrive(p, 1 - core, pl.ds(other, HALF), pre_recv)

    c_copy.wait()
    first_chunk = lax.div(lax.rem(z + 4, TP), 2)

    def chunk_state(i, carry):
        k = lax.rem(first_chunk + i, chunks)
        state = sloc_ref[pl.ds(pl.multiple_of(k * STATE, STATE), STATE), :] + sc_ref[pl.ds(12 + k, 1), :] * start_ref[...]
        us_ref[pl.ds(pl.multiple_of((2 * k + 1) * CHUNK, CHUNK), CHUNK), :] = (sc_ref[pl.ds(4 + k, 1), :] * state).astype(BF16)
        return carry

    def norm_block(i, carry):
        away = 4 - lax.div(i + 1, 2)
        step = jnp.where(lax.rem(i, 2) == 0, TP - away, away)
        block = lax.rem(z + step, TP)
        k = lax.div(block, 2)
        rows = pl.ds(pl.multiple_of(block * BLOCK, BLOCK), BLOCK)
        c = c_ref[rows, :]
        scores = nt(c, b_ref[pl.ds(pl.multiple_of(k * CHUNK, CHUNK), CHUNK), :])
        t = lax.rem(block, 2) * BLOCK + iota((BLOCK, CHUNK), 0)
        scores = jnp.where(t >= iota((BLOCK, CHUNK), 1), scores, 0.0).astype(BF16)
        ssm = nn(jnp.concatenate([scores, c], axis=1), us_ref[pl.ds(pl.multiple_of(k * 2 * CHUNK, CHUNK), 2 * CHUNK), :])
        mixed = ssm * ga_ref[rows, :] + gx_ref[rows, :]
        meansq = jnp.sum(mixed * mixed, axis=1, keepdims=True) * (1.0 / CHAN)
        n_ref[rows, :] = (mixed * lax.rsqrt(meansq + 1e-05) * gain_ref[...]).astype(BF16)
        return carry

    def project(unit, side, j):
        away = 4 - unit
        blocks = [lax.rem(z + away, TP)] if away in (0, 4) else [lax.rem(z + away, TP), lax.rem(z + TP - away, TP)]
        parts = [n_ref[pl.ds(pl.multiple_of(b * BLOCK, BLOCK), BLOCK), :] for b in blocks]
        rows = parts[0] if len(parts) == 1 else jnp.concatenate(parts, axis=0)
        here = pl.ds(pl.multiple_of(side * SIDE + j * SUBW, SUBW), SUBW)
        pr_ref[unit % 2, 0 : len(parts) * BLOCK, here] = nn(rows, w_ref[:, here])

    def ring_copy(s, d, j):
        return pltpu.make_async_remote_copy(
            src_ref=rs_send.at[s, d, j], dst_ref=rs_recv.at[s, d, j],
            send_sem=rs_ss.at[s, d, j], recv_sem=rs_rs.at[s, d, j],
            device_id={"tp": ring[d]}, device_id_type=pl.DeviceIdType.MESH,
        )

    sends = [(4, 0), (3, 1), (3, 0), (2, 1), (2, 0), (1, 1), (1, 0)]

    def ring_piece(s, d, j):
        away, near = sends[s]
        side = d ^ near
        low = BLOCK if d and away < 4 else 0
        lanes = pl.ds(pl.multiple_of(side * SIDE + j * SUBW, SUBW), SUBW)
        value = pr_ref[(4 - away) % 2, low : low + BLOCK, lanes]
        if s > 1:
            ring_copy(s - 2, d, j).wait_recv()
            value = value + rs_recv[s - 2, d, j].astype(F32)
        rs_send[s, d, j] = value.astype(BF16)
        ring_copy(s, d, j).start()

    def ring_step(s):
        def pieces(j, carry):
            if s < 2:
                for side in (range(2) if s == 0 else (1, 0)):
                    project(s, side, j)
                    ring_piece(s, side if s == 0 else 1 - side, j)
            else:
                for d in range(2):
                    ring_piece(s, d, j)
                    if s % 2 == 0:
                        project(s // 2 + 1, d, j)
            return carry

        lax.fori_loop(0, SUB, pieces, 0)

    def home(j, carry):
        for side in range(2):
            lanes = pl.ds(pl.multiple_of(side * SIDE + j * SUBW, SUBW), SUBW)
            value = pr_ref[0, 0:BLOCK, lanes]
            for s in (5, 6):
                d = side if s == 6 else 1 - side
                ring_copy(s, d, j).wait_recv()
                value = value + rs_recv[s, d, j].astype(F32)
            o_ref[:, lanes] = value.astype(BF16)
        return carry

    lax.fori_loop(0, 1, chunk_state, 0)
    lax.fori_loop(0, 1, norm_block, 0)
    w_copy.wait()
    ring_step(0)
    lax.fori_loop(1, chunks, chunk_state, 0)
    lax.fori_loop(1, 3, norm_block, 0)
    ring_step(1)
    lax.fori_loop(3, 5, norm_block, 0)
    ring_step(2)
    lax.fori_loop(5, TP, norm_block, 0)
    for s in range(3, TP - 1):
        ring_step(s)
    lax.fori_loop(0, SUB, home, 0)

    for copy in e_copies:
        copy.wait_send()
    for p in range(PIECES):
        pre_copy(p).wait_send()
    for l in range(LEVELS - 1):
        for p in range(PIECES):
            level_copy(l, p).wait_send()

    @pl.when(later[last] == 0)
    def _():
        for p in range(PIECES):
            level_copy(last, p).wait_send()

    for s in range(TP - 1):
        for d in range(2):
            for j in range(SUB):
                ring_copy(s, d, j).wait_send()


def on_device(x_in, gate_z, b_in, c_in, step_size, log_decay, skip, norm_gain, out_weight):
    vmem = pl.BlockSpec(memory_space=pltpu.VMEM)
    hbm = pl.BlockSpec(memory_space=pltpu.HBM)
    dma = pltpu.SemaphoreType.DMA
    return pl.pallas_call(
        kernel,
        out_shape=jax.ShapeDtypeStruct((BLOCK, DOUT), BF16),
        in_specs=[hbm] * 9,
        out_specs=vmem,
        scratch_shapes=[
            pltpu.VMEM((ROWS, CHAN), BF16),
            pltpu.VMEM((ROWS, STATE), BF16),
            pltpu.VMEM((HEADS, ROWS), F32),
            pltpu.VMEM((HEADS, ROWS), F32),
            pltpu.VMEM((1, HEADS), F32),
            pltpu.VMEM((1, CHAN), F32),
            pltpu.VMEM((ROWS, STATE), BF16),
            pltpu.VMEM((ROWS, CHAN), BF16),
            pltpu.VMEM((CHAN, DOUT), BF16),
            pltpu.VMEM((64, CHUNK), F32),
            pltpu.VMEM((64, CHUNK), F32),
            pltpu.VMEM((32, CHAN), F32),
            pltpu.VMEM((2 * ROWS, CHAN), BF16),
            pltpu.VMEM((STATE, CHAN), F32),
            pltpu.VMEM((4 * STATE, CHAN), F32),
            pltpu.VMEM((ROWS, CHAN), F32),
            pltpu.VMEM((ROWS, CHAN), F32),
            pltpu.VMEM((2, HEAD_ROWS + STATE, HALF), BF16),
            pltpu.VMEM((2, HEAD_ROWS + STATE, HALF), BF16),
            pltpu.VMEM((LEVELS, HEAD_ROWS + STATE, HALF), BF16),
            pltpu.VMEM((LEVELS, HEAD_ROWS + STATE, HALF), BF16),
            pltpu.VMEM((STATE, HALF), F32),
            pltpu.VMEM((STATE, HALF), F32),
            pltpu.VMEM((STATE, HALF), BF16),
            pltpu.VMEM((STATE, HALF), BF16),
            pltpu.VMEM((STATE, CHAN), F32),
            pltpu.VMEM((ROWS, CHAN), BF16),
            pltpu.VMEM((2, 2 * BLOCK, DOUT), F32),
            pltpu.VMEM((TP - 1, 2, SUB, BLOCK, SUBW), BF16),
            pltpu.VMEM((TP - 1, 2, SUB, BLOCK, SUBW), BF16),
            dma((4,)), dma((5,)), dma, dma, dma,
            dma((2,)), dma((2,)),
            dma((LEVELS, PIECES)), dma((LEVELS, PIECES)),
            dma((PIECES,)), dma((PIECES,)),
            dma((TP - 1, 2, SUB)), dma((TP - 1, 2, SUB)),
        ],
        compiler_params=pltpu.CompilerParams(
            collective_id=0, has_side_effects=True, vmem_limit_bytes=44 * 1024 * 1024
        ),
        name="state_space_layer",
    )(
        *[
            pltpu.with_memory_space_constraint(a, pltpu.HBM)
            for a in (
                x_in, b_in, step_size.T, log_decay.T, skip.reshape(1, HEADS), norm_gain.reshape(1, CHAN),
                gate_z, c_in, out_weight,
            )
        ]
    )


def solution(mesh):
    placed = (
        P("ctx", "tp"),
        P("ctx", "tp"),
        P("ctx", "tp"),
        P("ctx", "tp"),
        P("ctx", "tp"),
        P("ctx", "tp"),
        P("tp"),
        P("tp"),
        P("tp", None),
    )
    return jax.shard_map(
        on_device, mesh=mesh, in_specs=placed, out_specs=P(("ctx", "tp"), None), check_vma=False
    )
```

```python
import jax
import jax.numpy as jnp
from jax import lax
from jax.experimental import pallas as pl
from jax.experimental.pallas import tpu as pltpu
from jax.sharding import PartitionSpec as P

F32 = jnp.float32
BF16 = jnp.bfloat16
HEADS = 16
HEAD_DIM = 64
STATE = 128
CHUNK = 128
ROWS = 512
CHAN = 1024
HALF = CHAN // 2
DOUT = 4096
TP = 8
BLOCK = ROWS // TP
SIDE = DOUT // 2
SUB = 2
SUBW = SIDE // SUB
LEVELS = 4
PIECES = 8
PROWS = STATE // PIECES
HEAD_ROWS = 16


def iota(shape, dim):
    return lax.broadcasted_iota(jnp.int32, shape, dim)


def split2(v):
    high = v.astype(BF16)
    return high, (v - high.astype(F32)).astype(BF16)


def nn(a, b):
    return lax.dot_general(a, b, (((1,), (0,)), ((), ())), preferred_element_type=F32)


def nt(a, b):
    return lax.dot_general(a, b, (((1,), (1,)), ((), ())), preferred_element_type=F32)


def tn(a, b):
    return lax.dot_general(a, b, (((0,), (0,)), ((), ())), preferred_element_type=F32)


def per_channel(by_head, expand):
    return tn(jnp.concatenate(split2(by_head), axis=0), expand)


def decay_rows(row):
    high, low = split2(row)
    shape = (HEAD_ROWS // 2, row.shape[1])
    both = [jnp.broadcast_to(v.astype(F32), shape) for v in (high, low)]
    return jnp.concatenate(both, axis=0).astype(BF16)


def decay_of(tile):
    tile = tile.astype(F32)
    return tile[0:1] + tile[HEAD_ROWS // 2 : HEAD_ROWS // 2 + 1]


def kernel(
    x_hbm, b_hbm, dt_hbm, ld_hbm, skip_hbm, gain_hbm, z_hbm, c_hbm, w_hbm,
    o_ref,
    x_ref, b_ref, dt_ref, ld_ref, skip_ref, gain_ref, c_ref, z_ref, w_ref, wa_ref, wb_ref, sc_ref, us_ref, s_ref, sloc_ref, ga_ref, gx_ref,
    e_send, e_recv, lv_send, lv_recv, t_ref, p_ref, pre_send, pre_recv,
    start_ref, n_ref, pr_ref, rs_send, rs_recv,
    x_sem, small_sem, c_sem, z_sem, w_sem, e_ss, e_rs, lv_ss, lv_rs, pre_ss, pre_rs, rs_ss, rs_rs,
):
    ctx = lax.axis_index("ctx")
    z = lax.axis_index("tp")
    core = lax.rem(ctx, 2)
    y = lax.rem(lax.div(ctx, 2), 4)
    x = lax.div(ctx, 8)
    peer = ctx + 1 - 2 * core
    partners = [
        ctx + 2 * (1 - 2 * lax.rem(y, 2)),
        ctx + 2 * (3 - 2 * y),
        ctx + 8 * (1 - 2 * lax.rem(x, 2)),
        ctx + 8 * (3 - 2 * x),
    ]
    later = [lax.rem(y, 2), lax.div(y, 2), lax.rem(x, 2), lax.div(x, 2)]
    ring = [lax.rem(z + 1, TP), lax.rem(z + TP - 1, TP)]
    mine = pl.multiple_of(core * HALF, HALF)
    other = pl.multiple_of((1 - core) * HALF, HALF)

    barrier = pltpu.get_barrier_semaphore()
    for c in [peer] + partners:
        pl.semaphore_signal(barrier, inc=1, device_id={"ctx": c}, device_id_type=pl.DeviceIdType.MESH)
    for t in ring:
        pl.semaphore_signal(barrier, inc=1, device_id={"tp": t}, device_id_type=pl.DeviceIdType.MESH)

    small = [(ld_hbm, ld_ref), (dt_hbm, dt_ref), (b_hbm, b_ref), (skip_hbm, skip_ref), (gain_hbm, gain_ref)]
    small = [pltpu.make_async_copy(a, b, small_sem.at[i]) for i, (a, b) in enumerate(small)]
    for copy in small[:3]:
        copy.start()
    chunks = ROWS // CHUNK
    x_copies = []
    for k in range(chunks):
        rows = pl.ds(k * CHUNK, CHUNK)
        copy = pltpu.make_async_copy(x_hbm.at[rows, :], x_ref.at[rows, :], x_sem.at[k])
        copy.start()
        x_copies.append(copy)
    z_copy = pltpu.make_async_copy(z_hbm, z_ref, z_sem)
    z_copy.start()
    for copy in small[3:]:
        copy.start()
    c_copy = pltpu.make_async_copy(c_hbm, c_ref, c_sem)
    c_copy.start()
    w_copy = pltpu.make_async_copy(w_hbm, w_ref, w_sem)

    lane = iota((HEADS, CHAN), 1)
    first = iota((HEADS, CHAN), 0) * HEAD_DIM
    one_head = jnp.where((lane >= first) & (lane < first + HEAD_DIM), 1.0, 0.0).astype(BF16)
    expand = jnp.concatenate([one_head, one_head], axis=0)
    upper = jnp.where(iota((CHUNK, CHUNK), 0) <= iota((CHUNK, CHUNK), 1), 1.0, 0.0).astype(BF16)

    def stack(ref):
        return jnp.concatenate([ref[:, k * CHUNK : (k + 1) * CHUNK] for k in range(chunks)], axis=0)

    small[0].wait()
    log_decay = stack(ld_ref)
    high, low = split2(log_decay)
    rest = ((log_decay - high.astype(F32)) - low.astype(F32)).astype(BF16)
    run = nn(high, upper) + nn(low, upper) + nn(rest, upper)
    middle = jnp.broadcast_to(run[:, CHUNK // 2 - 1 : CHUNK // 2], run.shape)
    total = jnp.broadcast_to(run[:, CHUNK - 1 : CHUNK], run.shape)
    wa_ref[...] = jnp.exp(run - middle)
    small[1].wait()
    wb_ref[...] = jnp.exp(middle - run) * stack(dt_ref)
    column = iota((HEADS, CHUNK), 1)
    logs = jnp.zeros((HEADS, CHUNK), F32)
    before = jnp.zeros((HEADS, CHUNK), F32)
    for k in range(chunks):
        mid_k = middle[k * HEADS : (k + 1) * HEADS]
        tot_k = total[k * HEADS : (k + 1) * HEADS]
        logs = jnp.where(column == k, tot_k - mid_k, logs)
        logs = jnp.where(column == 4 + k, mid_k, logs)
        logs = jnp.where(column == 8 + k, tot_k, logs)
        logs = jnp.where(column == 12 + k, before, logs)
        before = before + tot_k
    logs = jnp.where(column == 16, before, logs)
    sc_ref[...] = per_channel(jnp.exp(logs), expand)[0:32]
    small[2].wait()
    for k in range(chunks):
        rows = slice(k * CHUNK, (k + 1) * CHUNK)
        factor = per_channel(wb_ref[k * HEADS : (k + 1) * HEADS, :], expand)
        x_copies[k].wait()
        u = (x_ref[rows, :].astype(F32) * factor).astype(BF16)
        us_ref[2 * k * CHUNK : (2 * k + 1) * CHUNK, :] = u
        fresh = sc_ref[k : k + 1, :] * tn(b_ref[rows, :], u)
        if k == 0:
            s_ref[...] = fresh
        else:
            state = s_ref[...]
            sloc_ref[k * STATE : (k + 1) * STATE, :] = state
            s_ref[...] = sc_ref[8 + k : 9 + k, :] * state + fresh
    sloc_ref[0:STATE, :] = jnp.zeros((STATE, CHAN), F32)
    w_copy.start()

    pl.semaphore_wait(barrier, 7)

    cut = HEAD_ROWS + STATE // 4
    part = [pl.ds(0, cut), pl.ds(cut, HEAD_ROWS + STATE - cut), pl.ds(0, HEAD_ROWS + STATE)]

    def to_peer(h, slot):
        return pltpu.make_async_remote_copy(
            src_ref=e_send.at[h, part[slot], :], dst_ref=e_recv.at[h, part[slot], :], send_sem=e_ss.at[slot], recv_sem=e_rs.at[slot],
            device_id={"ctx": peer}, device_id_type=pl.DeviceIdType.MESH,
        )

    e_copies = []
    for h, lanes, slots in [(1 - core, pl.ds(other, HALF), (0, 1)), (core, pl.ds(mine, HALF), (2,))]:
        e_send[h, 0:HEAD_ROWS, :] = decay_rows(sc_ref[16:17, lanes])
        for slot in slots:
            low, high = [(0, cut - HEAD_ROWS), (cut - HEAD_ROWS, STATE), (0, STATE)][slot]
            e_send[h, HEAD_ROWS + low : HEAD_ROWS + high, :] = s_ref[low:high, lanes].astype(BF16)
            copy = to_peer(h, slot)
            copy.start()
            e_copies.append(copy)

    for copy in small[3:]:
        copy.wait()
    skip_row = nn(jnp.concatenate(split2(skip_ref[...]), axis=1), expand)

    def gate(k):
        rows = slice(k * CHUNK, (k + 1) * CHUNK)
        after = per_channel(wa_ref[k * HEADS : (k + 1) * HEADS, :], expand)
        v = z_ref[rows, :].astype(F32)
        gated = v / (1.0 + jnp.exp(-v))
        ga_ref[rows, :] = after * gated
        gx_ref[rows, :] = skip_row * x_ref[rows, :].astype(F32) * gated

    to_peer(core, 0).wait_recv()
    is_late = core == 1
    d_mine = sc_ref[16:17, pl.ds(mine, HALF)]
    d_peer = decay_of(e_recv[core, 0:HEAD_ROWS, :])
    block_decay = d_mine * d_peer
    scale_mine = jnp.where(is_late, 1.0, d_peer)
    scale_peer = jnp.where(is_late, d_mine, 1.0)

    def piece_rows(p):
        return pl.ds(pl.multiple_of(p * PROWS, PROWS), PROWS)

    def held(p):
        return pl.ds(pl.multiple_of(HEAD_ROWS + p * PROWS, PROWS), PROWS)

    def level_copy(l, p):
        first = isinstance(p, int) and p == 0
        rows = pl.ds(0, HEAD_ROWS + PROWS) if first else held(p)
        return pltpu.make_async_remote_copy(
            src_ref=lv_send.at[l, rows, :], dst_ref=lv_recv.at[l, rows, :],
            send_sem=lv_ss.at[l, p], recv_sem=lv_rs.at[l, p],
            device_id={"ctx": partners[l]}, device_id_type=pl.DeviceIdType.MESH,
        )

    def send_level(l, p, state, decay):
        if isinstance(p, int) and p == 0:
            lv_send[l, 0:HEAD_ROWS, :] = decay_rows(decay)
        lv_send[l, held(p), :] = state.astype(BF16)
        if l < LEVELS - 1:
            level_copy(l, p).start()
        else:

            @pl.when(later[l] == 0)
            def _():
                level_copy(l, p).start()

    def first_piece(p):
        theirs = e_recv[core, held(p), :].astype(F32)
        state = scale_mine * s_ref[piece_rows(p), pl.ds(mine, HALF)] + scale_peer * theirs
        t_ref[piece_rows(p), :] = state
        send_level(0, p, state, block_decay)

    def every_piece(body):
        body(0)

        def later_piece(p, carry):
            body(p)
            return carry

        lax.fori_loop(1, PIECES, later_piece, 0)

    def first_pieces(p, carry):
        first_piece(p)
        return carry

    first_piece(0)
    lax.fori_loop(1, PIECES // 4, first_pieces, 0)
    to_peer(core, 1).wait_recv()
    lax.fori_loop(PIECES // 4, PIECES, first_pieces, 0)

    def pre_copy(p):
        rows = piece_rows(p)
        return pltpu.make_async_remote_copy(
            src_ref=pre_send.at[rows, :], dst_ref=pre_recv.at[rows, :], send_sem=pre_ss.at[p], recv_sem=pre_rs.at[p],
            device_id={"ctx": peer}, device_id_type=pl.DeviceIdType.MESH,
        )

    z_copy.wait()
    prefix_decay = jnp.ones((1, HALF), F32)
    for l in range(LEVELS - 1):
        gate(l)
        up = later[l] == 1
        level_copy(l, 0).wait_recv()
        their_decay = decay_of(lv_recv[l, 0:HEAD_ROWS, :])
        to_prefix = jnp.where(up, prefix_decay, 0.0)
        scale_theirs = jnp.where(up, block_decay, 1.0)
        scale_ours = jnp.where(up, 1.0, their_decay)
        next_decay = block_decay * their_decay

        def level_piece(p):
            if not isinstance(p, int):
                level_copy(l, p).wait_recv()
            rows = piece_rows(p)
            theirs = lv_recv[l, held(p), :].astype(F32)
            state = scale_theirs * theirs + scale_ours * t_ref[rows, :]
            t_ref[rows, :] = state
            send_level(l + 1, p, state, next_decay)
            gain = to_prefix * theirs
            p_ref[rows, :] = gain if l == 0 else p_ref[rows, :] + gain

        every_piece(level_piece)
        prefix_decay = jnp.where(up, prefix_decay * their_decay, prefix_decay)
        block_decay = next_decay

    last = LEVELS - 1
    gate(last)
    def last_piece(p):
        rows = piece_rows(p)

        @pl.when(later[last] == 1)
        def _():
            level_copy(last, p).wait_recv()
            theirs = lv_recv[last, held(p), :].astype(F32)
            p_ref[rows, :] = p_ref[rows, :] + prefix_decay * theirs

        pre_send[rows, :] = p_ref[rows, :].astype(BF16)
        pre_copy(p).start()

    every_piece(last_piece)

    to_peer(1 - core, 2).wait_recv()

    def arrive(p, h, lanes, ref):
        piece = piece_rows(p)
        theirs = e_recv[h, held(p), :].astype(F32)
        decay = decay_of(e_recv[h, 0:HEAD_ROWS, :])
        start = jnp.where(is_late, decay, 1.0) * ref[piece, :].astype(F32) + jnp.where(is_late, theirs, 0.0)
        start_ref[piece, lanes] = start

    def own_half(p, carry):
        arrive(p, core, pl.ds(mine, HALF), pre_send)
        return carry

    def other_half(p, carry):
        pre_copy(p).wait_recv()
        arrive(p, 1 - core, pl.ds(other, HALF), pre_recv)
        return carry

    lax.fori_loop(0, PIECES, own_half, 0)
    lax.fori_loop(0, PIECES, other_half, 0)

    c_copy.wait()
    first_chunk = lax.div(lax.rem(z + 4, TP), 2)

    def chunk_state(i, carry):
        k = lax.rem(first_chunk + i, chunks)
        state = sloc_ref[pl.ds(pl.multiple_of(k * STATE, STATE), STATE), :] + sc_ref[pl.ds(12 + k, 1), :] * start_ref[...]
        us_ref[pl.ds(pl.multiple_of((2 * k + 1) * CHUNK, CHUNK), CHUNK), :] = (sc_ref[pl.ds(4 + k, 1), :] * state).astype(BF16)
        return carry

    def norm_block(i, carry):
        away = 4 - lax.div(i + 1, 2)
        step = jnp.where(lax.rem(i, 2) == 0, TP - away, away)
        block = lax.rem(z + step, TP)
        k = lax.div(block, 2)
        rows = pl.ds(pl.multiple_of(block * BLOCK, BLOCK), BLOCK)
        c = c_ref[rows, :]
        scores = nt(c, b_ref[pl.ds(pl.multiple_of(k * CHUNK, CHUNK), CHUNK), :])
        t = lax.rem(block, 2) * BLOCK + iota((BLOCK, CHUNK), 0)
        scores = jnp.where(t >= iota((BLOCK, CHUNK), 1), scores, 0.0).astype(BF16)
        ssm = nn(jnp.concatenate([scores, c], axis=1), us_ref[pl.ds(pl.multiple_of(k * 2 * CHUNK, CHUNK), 2 * CHUNK), :])
        mixed = ssm * ga_ref[rows, :] + gx_ref[rows, :]
        meansq = jnp.sum(mixed * mixed, axis=1, keepdims=True) * (1.0 / CHAN)
        n_ref[rows, :] = (mixed * lax.rsqrt(meansq + 1e-05) * gain_ref[...]).astype(BF16)
        return carry

    def project(unit, side, j):
        away = 4 - unit
        blocks = [lax.rem(z + away, TP)] if away in (0, 4) else [lax.rem(z + away, TP), lax.rem(z + TP - away, TP)]
        parts = [n_ref[pl.ds(pl.multiple_of(b * BLOCK, BLOCK), BLOCK), :] for b in blocks]
        rows = parts[0] if len(parts) == 1 else jnp.concatenate(parts, axis=0)
        here = pl.ds(pl.multiple_of(side * SIDE + j * SUBW, SUBW), SUBW)
        pr_ref[unit % 2, 0 : len(parts) * BLOCK, here] = nn(rows, w_ref[:, here])

    def ring_copy(s, d, j):
        return pltpu.make_async_remote_copy(
            src_ref=rs_send.at[s, d, j], dst_ref=rs_recv.at[s, d, j],
            send_sem=rs_ss.at[s, d, j], recv_sem=rs_rs.at[s, d, j],
            device_id={"tp": ring[d]}, device_id_type=pl.DeviceIdType.MESH,
        )

    sends = [(4, 0), (3, 1), (3, 0), (2, 1), (2, 0), (1, 1), (1, 0)]

    def ring_piece(s, d, j):
        away, near = sends[s]
        side = d ^ near
        low = BLOCK if d and away < 4 else 0
        lanes = pl.ds(pl.multiple_of(side * SIDE + j * SUBW, SUBW), SUBW)
        value = pr_ref[(4 - away) % 2, low : low + BLOCK, lanes]
        if s > 1:
            ring_copy(s - 2, d, j).wait_recv()
            value = value + rs_recv[s - 2, d, j].astype(F32)
        rs_send[s, d, j] = value.astype(BF16)
        ring_copy(s, d, j).start()

    def ring_step(s):
        def pieces(j, carry):
            if s < 2:
                for side in (range(2) if s == 0 else (1, 0)):
                    project(s, side, j)
                    ring_piece(s, side if s == 0 else 1 - side, j)
            else:
                for d in range(2):
                    ring_piece(s, d, j)
                    if s % 2 == 0:
                        project(s // 2 + 1, d, j)
            return carry

        lax.fori_loop(0, SUB, pieces, 0)

    def home(j, carry):
        for side in range(2):
            lanes = pl.ds(pl.multiple_of(side * SIDE + j * SUBW, SUBW), SUBW)
            value = pr_ref[0, 0:BLOCK, lanes]
            for s in (5, 6):
                d = side if s == 6 else 1 - side
                ring_copy(s, d, j).wait_recv()
                value = value + rs_recv[s, d, j].astype(F32)
            o_ref[:, lanes] = value.astype(BF16)
        return carry

    lax.fori_loop(0, 1, chunk_state, 0)
    lax.fori_loop(0, 1, norm_block, 0)
    w_copy.wait()
    ring_step(0)
    lax.fori_loop(1, chunks, chunk_state, 0)
    lax.fori_loop(1, 3, norm_block, 0)
    ring_step(1)
    lax.fori_loop(3, 5, norm_block, 0)
    ring_step(2)
    lax.fori_loop(5, TP, norm_block, 0)
    for s in range(3, TP - 1):
        ring_step(s)
    lax.fori_loop(0, SUB, home, 0)

    for copy in e_copies:
        copy.wait_send()
    for p in range(PIECES):
        pre_copy(p).wait_send()
    for l in range(LEVELS - 1):
        for p in range(PIECES):
            level_copy(l, p).wait_send()

    @pl.when(later[last] == 0)
    def _():
        for p in range(PIECES):
            level_copy(last, p).wait_send()

    for s in range(TP - 1):
        for d in range(2):
            for j in range(SUB):
                ring_copy(s, d, j).wait_send()


def on_device(x_in, gate_z, b_in, c_in, step_size, log_decay, skip, norm_gain, out_weight):
    vmem = pl.BlockSpec(memory_space=pltpu.VMEM)
    hbm = pl.BlockSpec(memory_space=pltpu.HBM)
    dma = pltpu.SemaphoreType.DMA
    return pl.pallas_call(
        kernel,
        out_shape=jax.ShapeDtypeStruct((BLOCK, DOUT), BF16),
        in_specs=[hbm] * 9,
        out_specs=vmem,
        scratch_shapes=[
            pltpu.VMEM((ROWS, CHAN), BF16),
            pltpu.VMEM((ROWS, STATE), BF16),
            pltpu.VMEM((HEADS, ROWS), F32),
            pltpu.VMEM((HEADS, ROWS), F32),
            pltpu.VMEM((1, HEADS), F32),
            pltpu.VMEM((1, CHAN), F32),
            pltpu.VMEM((ROWS, STATE), BF16),
            pltpu.VMEM((ROWS, CHAN), BF16),
            pltpu.VMEM((CHAN, DOUT), BF16),
            pltpu.VMEM((64, CHUNK), F32),
            pltpu.VMEM((64, CHUNK), F32),
            pltpu.VMEM((32, CHAN), F32),
            pltpu.VMEM((2 * ROWS, CHAN), BF16),
            pltpu.VMEM((STATE, CHAN), F32),
            pltpu.VMEM((4 * STATE, CHAN), F32),
            pltpu.VMEM((ROWS, CHAN), F32),
            pltpu.VMEM((ROWS, CHAN), F32),
            pltpu.VMEM((2, HEAD_ROWS + STATE, HALF), BF16),
            pltpu.VMEM((2, HEAD_ROWS + STATE, HALF), BF16),
            pltpu.VMEM((LEVELS, HEAD_ROWS + STATE, HALF), BF16),
            pltpu.VMEM((LEVELS, HEAD_ROWS + STATE, HALF), BF16),
            pltpu.VMEM((STATE, HALF), F32),
            pltpu.VMEM((STATE, HALF), F32),
            pltpu.VMEM((STATE, HALF), BF16),
            pltpu.VMEM((STATE, HALF), BF16),
            pltpu.VMEM((STATE, CHAN), F32),
            pltpu.VMEM((ROWS, CHAN), BF16),
            pltpu.VMEM((2, 2 * BLOCK, DOUT), F32),
            pltpu.VMEM((TP - 1, 2, SUB, BLOCK, SUBW), BF16),
            pltpu.VMEM((TP - 1, 2, SUB, BLOCK, SUBW), BF16),
            dma((4,)), dma((5,)), dma, dma, dma,
            dma((3,)), dma((3,)),
            dma((LEVELS, PIECES)), dma((LEVELS, PIECES)),
            dma((PIECES,)), dma((PIECES,)),
            dma((TP - 1, 2, SUB)), dma((TP - 1, 2, SUB)),
        ],
        compiler_params=pltpu.CompilerParams(
            collective_id=0, has_side_effects=True, vmem_limit_bytes=44 * 1024 * 1024
        ),
        name="state_space_layer",
    )(
        *[
            pltpu.with_memory_space_constraint(a, pltpu.HBM)
            for a in (
                x_in, b_in, step_size.T, log_decay.T, skip.reshape(1, HEADS), norm_gain.reshape(1, CHAN),
                gate_z, c_in, out_weight,
            )
        ]
    )


def solution(mesh):
    placed = (
        P("ctx", "tp"),
        P("ctx", "tp"),
        P("ctx", "tp"),
        P("ctx", "tp"),
        P("ctx", "tp"),
        P("ctx", "tp"),
        P("tp"),
        P("tp"),
        P("tp", None),
    )
    return jax.shard_map(
        on_device, mesh=mesh, in_specs=placed, out_specs=P(("ctx", "tp"), None), check_vma=False
    )
```

```python
import jax
import jax.numpy as jnp
from jax import lax
from jax.experimental import pallas as pl
from jax.experimental.pallas import tpu as pltpu
from jax.sharding import PartitionSpec as P

F32 = jnp.float32
BF16 = jnp.bfloat16
HEADS = 16
HEAD_DIM = 64
STATE = 128
CHUNK = 128
ROWS = 512
CHAN = 1024
HALF = CHAN // 2
DOUT = 4096
TP = 8
BLOCK = ROWS // TP
SIDE = DOUT // 2
SUB = 2
SUBW = SIDE // SUB
LEVELS = 4
PIECES = 8
PROWS = STATE // PIECES
LAG = 4
HEAD_ROWS = 16


def iota(shape, dim):
    return lax.broadcasted_iota(jnp.int32, shape, dim)


def split2(v):
    high = v.astype(BF16)
    return high, (v - high.astype(F32)).astype(BF16)


def nn(a, b):
    return lax.dot_general(a, b, (((1,), (0,)), ((), ())), preferred_element_type=F32)


def nt(a, b):
    return lax.dot_general(a, b, (((1,), (1,)), ((), ())), preferred_element_type=F32)


def tn(a, b):
    return lax.dot_general(a, b, (((0,), (0,)), ((), ())), preferred_element_type=F32)


def per_channel(by_head, expand):
    return tn(jnp.concatenate(split2(by_head), axis=0), expand)


def decay_rows(row):
    high, low = split2(row)
    shape = (HEAD_ROWS // 2, row.shape[1])
    both = [jnp.broadcast_to(v.astype(F32), shape) for v in (high, low)]
    return jnp.concatenate(both, axis=0).astype(BF16)


def decay_of(tile):
    tile = tile.astype(F32)
    return tile[0:1] + tile[HEAD_ROWS // 2 : HEAD_ROWS // 2 + 1]


def kernel(
    x_hbm, b_hbm, dt_hbm, ld_hbm, skip_hbm, gain_hbm, z_hbm, c_hbm, w_hbm,
    o_ref,
    x_ref, b_ref, dt_ref, ld_ref, skip_ref, gain_ref, c_ref, z_ref, w_ref, wa_ref, wb_ref, sc_ref, us_ref, s_ref, sloc_ref, ga_ref, gx_ref,
    e_send, e_recv, lv_send, lv_recv, t_ref, p_ref, pre_send, pre_recv,
    start_ref, n_ref, pr_ref, rs_send, rs_recv,
    x_sem, small_sem, c_sem, z_sem, w_sem, e_ss, e_rs, lv_ss, lv_rs, pre_ss, pre_rs, rs_ss, rs_rs,
):
    ctx = lax.axis_index("ctx")
    z = lax.axis_index("tp")
    core = lax.rem(ctx, 2)
    y = lax.rem(lax.div(ctx, 2), 4)
    x = lax.div(ctx, 8)
    peer = ctx + 1 - 2 * core
    partners = [
        ctx + 2 * (1 - 2 * lax.rem(y, 2)),
        ctx + 2 * (3 - 2 * y),
        ctx + 8 * (1 - 2 * lax.rem(x, 2)),
        ctx + 8 * (3 - 2 * x),
    ]
    later = [lax.rem(y, 2), lax.div(y, 2), lax.rem(x, 2), lax.div(x, 2)]
    ring = [lax.rem(z + 1, TP), lax.rem(z + TP - 1, TP)]
    mine = pl.multiple_of(core * HALF, HALF)
    other = pl.multiple_of((1 - core) * HALF, HALF)

    barrier = pltpu.get_barrier_semaphore()
    for c in [peer] + partners:
        pl.semaphore_signal(barrier, inc=1, device_id={"ctx": c}, device_id_type=pl.DeviceIdType.MESH)
    for t in ring:
        pl.semaphore_signal(barrier, inc=1, device_id={"tp": t}, device_id_type=pl.DeviceIdType.MESH)

    small = [(ld_hbm, ld_ref), (dt_hbm, dt_ref), (b_hbm, b_ref), (skip_hbm, skip_ref), (gain_hbm, gain_ref)]
    small = [pltpu.make_async_copy(a, b, small_sem.at[i]) for i, (a, b) in enumerate(small)]
    for copy in small[:3]:
        copy.start()
    chunks = ROWS // CHUNK
    x_copies = []
    for k in range(chunks):
        rows = pl.ds(k * CHUNK, CHUNK)
        copy = pltpu.make_async_copy(x_hbm.at[rows, :], x_ref.at[rows, :], x_sem.at[k])
        copy.start()
        x_copies.append(copy)
    z_copy = pltpu.make_async_copy(z_hbm, z_ref, z_sem)
    z_copy.start()
    for copy in small[3:]:
        copy.start()
    c_copy = pltpu.make_async_copy(c_hbm, c_ref, c_sem)
    c_copy.start()
    w_copy = pltpu.make_async_copy(w_hbm, w_ref, w_sem)

    lane = iota((HEADS, CHAN), 1)
    first = iota((HEADS, CHAN), 0) * HEAD_DIM
    one_head = jnp.where((lane >= first) & (lane < first + HEAD_DIM), 1.0, 0.0).astype(BF16)
    expand = jnp.concatenate([one_head, one_head], axis=0)
    upper = jnp.where(iota((CHUNK, CHUNK), 0) <= iota((CHUNK, CHUNK), 1), 1.0, 0.0).astype(BF16)

    def stack(ref):
        return jnp.concatenate([ref[:, k * CHUNK : (k + 1) * CHUNK] for k in range(chunks)], axis=0)

    small[0].wait()
    log_decay = stack(ld_ref)
    high, low = split2(log_decay)
    rest = ((log_decay - high.astype(F32)) - low.astype(F32)).astype(BF16)
    run = nn(high, upper) + nn(low, upper) + nn(rest, upper)
    middle = jnp.broadcast_to(run[:, CHUNK // 2 - 1 : CHUNK // 2], run.shape)
    total = jnp.broadcast_to(run[:, CHUNK - 1 : CHUNK], run.shape)
    wa_ref[...] = jnp.exp(run - middle)
    small[1].wait()
    wb_ref[...] = jnp.exp(middle - run) * stack(dt_ref)
    column = iota((HEADS, CHUNK), 1)
    logs = jnp.zeros((HEADS, CHUNK), F32)
    before = jnp.zeros((HEADS, CHUNK), F32)
    for k in range(chunks):
        mid_k = middle[k * HEADS : (k + 1) * HEADS]
        tot_k = total[k * HEADS : (k + 1) * HEADS]
        logs = jnp.where(column == k, tot_k - mid_k, logs)
        logs = jnp.where(column == 4 + k, mid_k, logs)
        logs = jnp.where(column == 8 + k, tot_k, logs)
        logs = jnp.where(column == 12 + k, before, logs)
        before = before + tot_k
    logs = jnp.where(column == 16, before, logs)
    sc_ref[...] = per_channel(jnp.exp(logs), expand)[0:32]
    small[2].wait()
    for k in range(chunks):
        rows = slice(k * CHUNK, (k + 1) * CHUNK)
        factor = per_channel(wb_ref[k * HEADS : (k + 1) * HEADS, :], expand)
        x_copies[k].wait()
        u = (x_ref[rows, :].astype(F32) * factor).astype(BF16)
        us_ref[2 * k * CHUNK : (2 * k + 1) * CHUNK, :] = u
        fresh = sc_ref[k : k + 1, :] * tn(b_ref[rows, :], u)
        if k == 0:
            s_ref[...] = fresh
        else:
            state = s_ref[...]
            sloc_ref[k * STATE : (k + 1) * STATE, :] = state
            s_ref[...] = sc_ref[8 + k : 9 + k, :] * state + fresh
    sloc_ref[0:STATE, :] = jnp.zeros((STATE, CHAN), F32)
    w_copy.start()

    pl.semaphore_wait(barrier, 7)

    def to_peer(h, slot):
        return pltpu.make_async_remote_copy(
            src_ref=e_send.at[h], dst_ref=e_recv.at[h], send_sem=e_ss.at[slot], recv_sem=e_rs.at[slot],
            device_id={"ctx": peer}, device_id_type=pl.DeviceIdType.MESH,
        )

    e_copies = []
    for slot, (h, lanes) in enumerate([(1 - core, pl.ds(other, HALF)), (core, pl.ds(mine, HALF))]):
        e_send[h, 0:HEAD_ROWS, :] = decay_rows(sc_ref[16:17, lanes])
        e_send[h, HEAD_ROWS:, :] = s_ref[:, lanes].astype(BF16)
        copy = to_peer(h, slot)
        copy.start()
        e_copies.append(copy)

    for copy in small[3:]:
        copy.wait()
    skip_row = nn(jnp.concatenate(split2(skip_ref[...]), axis=1), expand)

    def gate(k):
        rows = slice(k * CHUNK, (k + 1) * CHUNK)
        after = per_channel(wa_ref[k * HEADS : (k + 1) * HEADS, :], expand)
        v = z_ref[rows, :].astype(F32)
        gated = v / (1.0 + jnp.exp(-v))
        ga_ref[rows, :] = after * gated
        gx_ref[rows, :] = skip_row * x_ref[rows, :].astype(F32) * gated

    to_peer(core, 0).wait_recv()
    is_late = core == 1
    d_mine = sc_ref[16:17, pl.ds(mine, HALF)]
    d_peer = decay_of(e_recv[core, 0:HEAD_ROWS, :])
    block_decay = d_mine * d_peer
    scale_mine = jnp.where(is_late, 1.0, d_peer)
    scale_peer = jnp.where(is_late, d_mine, 1.0)

    def level_copy(l, p):
        rows = slice(0 if p == 0 else HEAD_ROWS + p * PROWS, HEAD_ROWS + (p + 1) * PROWS)
        return pltpu.make_async_remote_copy(
            src_ref=lv_send.at[l, rows, :], dst_ref=lv_recv.at[l, rows, :],
            send_sem=lv_ss.at[l, p], recv_sem=lv_rs.at[l, p],
            device_id={"ctx": partners[l]}, device_id_type=pl.DeviceIdType.MESH,
        )

    def send_level(l, p, state, decay):
        if p == 0:
            lv_send[l, 0:HEAD_ROWS, :] = decay_rows(decay)
        lv_send[l, HEAD_ROWS + p * PROWS : HEAD_ROWS + (p + 1) * PROWS, :] = state.astype(BF16)
        if l < LEVELS - 1:
            level_copy(l, p).start()
        else:

            @pl.when(later[l] == 0)
            def _():
                level_copy(l, p).start()

    for p in range(PIECES):
        rows = slice(p * PROWS, (p + 1) * PROWS)
        theirs = e_recv[core, HEAD_ROWS + p * PROWS : HEAD_ROWS + (p + 1) * PROWS, :].astype(F32)
        state = scale_mine * s_ref[rows, pl.ds(mine, HALF)] + scale_peer * theirs
        t_ref[rows, :] = state
        send_level(0, p, state, block_decay)

    def pre_copy(p):
        rows = slice(p * PROWS, (p + 1) * PROWS)
        return pltpu.make_async_remote_copy(
            src_ref=pre_send.at[rows, :], dst_ref=pre_recv.at[rows, :], send_sem=pre_ss.at[p], recv_sem=pre_rs.at[p],
            device_id={"ctx": peer}, device_id_type=pl.DeviceIdType.MESH,
        )

    z_copy.wait()
    prefix_decay = jnp.ones((1, HALF), F32)
    for l in range(LEVELS - 1):
        gate(l)
        up = later[l] == 1
        for p in range(PIECES):
            rows = slice(p * PROWS, (p + 1) * PROWS)
            level_copy(l, p).wait_recv()
            if p == 0:
                their_decay = decay_of(lv_recv[l, 0:HEAD_ROWS, :])
                to_prefix = jnp.where(up, prefix_decay, 0.0)
                scale_theirs = jnp.where(up, block_decay, 1.0)
                scale_ours = jnp.where(up, 1.0, their_decay)
                next_decay = block_decay * their_decay
            theirs = lv_recv[l, HEAD_ROWS + p * PROWS : HEAD_ROWS + (p + 1) * PROWS, :].astype(F32)
            state = scale_theirs * theirs + scale_ours * t_ref[rows, :]
            t_ref[rows, :] = state
            send_level(l + 1, p, state, next_decay)
            gain = to_prefix * theirs
            p_ref[rows, :] = gain if l == 0 else p_ref[rows, :] + gain
        prefix_decay = jnp.where(up, prefix_decay * their_decay, prefix_decay)
        block_decay = next_decay

    last = LEVELS - 1
    gate(last)
    to_peer(1 - core, 1).wait_recv()
    first_chunk = lax.div(lax.rem(z + 4, TP), 2)

    def arrive(p, h, lanes, ref):
        piece = slice(p * PROWS, (p + 1) * PROWS)
        theirs = e_recv[h, HEAD_ROWS + p * PROWS : HEAD_ROWS + (p + 1) * PROWS, :].astype(F32)
        decay = decay_of(e_recv[h, 0:HEAD_ROWS, :])
        start = jnp.where(is_late, decay, 1.0) * ref[piece, :].astype(F32) + jnp.where(is_late, theirs, 0.0)
        start_ref[piece, lanes] = start
        k = first_chunk
        state = sloc_ref[pl.ds(pl.multiple_of(k * STATE + p * PROWS, PROWS), PROWS), lanes]
        state = sc_ref[pl.ds(4 + k, 1), lanes] * (state + sc_ref[pl.ds(12 + k, 1), lanes] * start)
        us_ref[pl.ds(pl.multiple_of((2 * k + 1) * CHUNK + p * PROWS, PROWS), PROWS), lanes] = state.astype(BF16)

    def arrive_other(p):
        pre_copy(p).wait_recv()
        arrive(p, 1 - core, pl.ds(other, HALF), pre_recv)

    for p in range(PIECES):
        rows = slice(p * PROWS, (p + 1) * PROWS)

        @pl.when(later[last] == 1)
        def _():
            level_copy(last, p).wait_recv()
            theirs = lv_recv[last, HEAD_ROWS + p * PROWS : HEAD_ROWS + (p + 1) * PROWS, :].astype(F32)
            p_ref[rows, :] = p_ref[rows, :] + prefix_decay * theirs

        pre_send[rows, :] = p_ref[rows, :].astype(BF16)
        pre_copy(p).start()
        arrive(p, core, pl.ds(mine, HALF), pre_send)
        if p >= LAG:
            arrive_other(p - LAG)
    for p in range(PIECES - LAG, PIECES):
        arrive_other(p)
    c_copy.wait()

    def chunk_state(i, carry):
        k = lax.rem(first_chunk + i, chunks)
        state = sloc_ref[pl.ds(pl.multiple_of(k * STATE, STATE), STATE), :] + sc_ref[pl.ds(12 + k, 1), :] * start_ref[...]
        us_ref[pl.ds(pl.multiple_of((2 * k + 1) * CHUNK, CHUNK), CHUNK), :] = (sc_ref[pl.ds(4 + k, 1), :] * state).astype(BF16)
        return carry

    def norm_block(i, carry):
        away = 4 - lax.div(i + 1, 2)
        step = jnp.where(lax.rem(i, 2) == 0, TP - away, away)
        block = lax.rem(z + step, TP)
        k = lax.div(block, 2)
        rows = pl.ds(pl.multiple_of(block * BLOCK, BLOCK), BLOCK)
        c = c_ref[rows, :]
        scores = nt(c, b_ref[pl.ds(pl.multiple_of(k * CHUNK, CHUNK), CHUNK), :])
        t = lax.rem(block, 2) * BLOCK + iota((BLOCK, CHUNK), 0)
        scores = jnp.where(t >= iota((BLOCK, CHUNK), 1), scores, 0.0).astype(BF16)
        ssm = nn(jnp.concatenate([scores, c], axis=1), us_ref[pl.ds(pl.multiple_of(k * 2 * CHUNK, CHUNK), 2 * CHUNK), :])
        mixed = ssm * ga_ref[rows, :] + gx_ref[rows, :]
        meansq = jnp.sum(mixed * mixed, axis=1, keepdims=True) * (1.0 / CHAN)
        n_ref[rows, :] = (mixed * lax.rsqrt(meansq + 1e-05) * gain_ref[...]).astype(BF16)
        return carry

    def project(unit, side, j):
        away = 4 - unit
        blocks = [lax.rem(z + away, TP)] if away in (0, 4) else [lax.rem(z + away, TP), lax.rem(z + TP - away, TP)]
        parts = [n_ref[pl.ds(pl.multiple_of(b * BLOCK, BLOCK), BLOCK), :] for b in blocks]
        rows = parts[0] if len(parts) == 1 else jnp.concatenate(parts, axis=0)
        here = pl.ds(pl.multiple_of(side * SIDE + j * SUBW, SUBW), SUBW)
        pr_ref[unit % 2, 0 : len(parts) * BLOCK, here] = nn(rows, w_ref[:, here])

    def ring_copy(s, d, j):
        return pltpu.make_async_remote_copy(
            src_ref=rs_send.at[s, d, j], dst_ref=rs_recv.at[s, d, j],
            send_sem=rs_ss.at[s, d, j], recv_sem=rs_rs.at[s, d, j],
            device_id={"tp": ring[d]}, device_id_type=pl.DeviceIdType.MESH,
        )

    sends = [(4, 0), (3, 1), (3, 0), (2, 1), (2, 0), (1, 1), (1, 0)]

    def ring_piece(s, d, j):
        away, near = sends[s]
        side = d ^ near
        low = BLOCK if d and away < 4 else 0
        lanes = pl.ds(pl.multiple_of(side * SIDE + j * SUBW, SUBW), SUBW)
        value = pr_ref[(4 - away) % 2, low : low + BLOCK, lanes]
        if s > 1:
            ring_copy(s - 2, d, j).wait_recv()
            value = value + rs_recv[s - 2, d, j].astype(F32)
        rs_send[s, d, j] = value.astype(BF16)
        ring_copy(s, d, j).start()

    def ring_step(s):
        def pieces(j, carry):
            if s < 2:
                for side in (range(2) if s == 0 else (1, 0)):
                    project(s, side, j)
                    ring_piece(s, side if s == 0 else 1 - side, j)
            else:
                for d in range(2):
                    ring_piece(s, d, j)
                    if s % 2 == 0:
                        project(s // 2 + 1, d, j)
            return carry

        lax.fori_loop(0, SUB, pieces, 0)

    def home(j, carry):
        for side in range(2):
            lanes = pl.ds(pl.multiple_of(side * SIDE + j * SUBW, SUBW), SUBW)
            value = pr_ref[0, 0:BLOCK, lanes]
            for s in (5, 6):
                d = side if s == 6 else 1 - side
                ring_copy(s, d, j).wait_recv()
                value = value + rs_recv[s, d, j].astype(F32)
            o_ref[:, lanes] = value.astype(BF16)
        return carry

    lax.fori_loop(0, 1, norm_block, 0)
    w_copy.wait()
    ring_step(0)
    lax.fori_loop(1, chunks, chunk_state, 0)
    lax.fori_loop(1, 3, norm_block, 0)
    ring_step(1)
    lax.fori_loop(3, 5, norm_block, 0)
    ring_step(2)
    lax.fori_loop(5, TP, norm_block, 0)
    for s in range(3, TP - 1):
        ring_step(s)
    lax.fori_loop(0, SUB, home, 0)

    for copy in e_copies:
        copy.wait_send()
    for p in range(PIECES):
        pre_copy(p).wait_send()
    for l in range(LEVELS - 1):
        for p in range(PIECES):
            level_copy(l, p).wait_send()

    @pl.when(later[last] == 0)
    def _():
        for p in range(PIECES):
            level_copy(last, p).wait_send()

    for s in range(TP - 1):
        for d in range(2):
            for j in range(SUB):
                ring_copy(s, d, j).wait_send()


def on_device(x_in, gate_z, b_in, c_in, step_size, log_decay, skip, norm_gain, out_weight):
    vmem = pl.BlockSpec(memory_space=pltpu.VMEM)
    hbm = pl.BlockSpec(memory_space=pltpu.HBM)
    dma = pltpu.SemaphoreType.DMA
    return pl.pallas_call(
        kernel,
        out_shape=jax.ShapeDtypeStruct((BLOCK, DOUT), BF16),
        in_specs=[hbm] * 9,
        out_specs=vmem,
        scratch_shapes=[
            pltpu.VMEM((ROWS, CHAN), BF16),
            pltpu.VMEM((ROWS, STATE), BF16),
            pltpu.VMEM((HEADS, ROWS), F32),
            pltpu.VMEM((HEADS, ROWS), F32),
            pltpu.VMEM((1, HEADS), F32),
            pltpu.VMEM((1, CHAN), F32),
            pltpu.VMEM((ROWS, STATE), BF16),
            pltpu.VMEM((ROWS, CHAN), BF16),
            pltpu.VMEM((CHAN, DOUT), BF16),
            pltpu.VMEM((64, CHUNK), F32),
            pltpu.VMEM((64, CHUNK), F32),
            pltpu.VMEM((32, CHAN), F32),
            pltpu.VMEM((2 * ROWS, CHAN), BF16),
            pltpu.VMEM((STATE, CHAN), F32),
            pltpu.VMEM((4 * STATE, CHAN), F32),
            pltpu.VMEM((ROWS, CHAN), F32),
            pltpu.VMEM((ROWS, CHAN), F32),
            pltpu.VMEM((2, HEAD_ROWS + STATE, HALF), BF16),
            pltpu.VMEM((2, HEAD_ROWS + STATE, HALF), BF16),
            pltpu.VMEM((LEVELS, HEAD_ROWS + STATE, HALF), BF16),
            pltpu.VMEM((LEVELS, HEAD_ROWS + STATE, HALF), BF16),
            pltpu.VMEM((STATE, HALF), F32),
            pltpu.VMEM((STATE, HALF), F32),
            pltpu.VMEM((STATE, HALF), BF16),
            pltpu.VMEM((STATE, HALF), BF16),
            pltpu.VMEM((STATE, CHAN), F32),
            pltpu.VMEM((ROWS, CHAN), BF16),
            pltpu.VMEM((2, 2 * BLOCK, DOUT), F32),
            pltpu.VMEM((TP - 1, 2, SUB, BLOCK, SUBW), BF16),
            pltpu.VMEM((TP - 1, 2, SUB, BLOCK, SUBW), BF16),
            dma((4,)), dma((5,)), dma, dma, dma,
            dma((2,)), dma((2,)),
            dma((LEVELS, PIECES)), dma((LEVELS, PIECES)),
            dma((PIECES,)), dma((PIECES,)),
            dma((TP - 1, 2, SUB)), dma((TP - 1, 2, SUB)),
        ],
        compiler_params=pltpu.CompilerParams(
            collective_id=0, has_side_effects=True, vmem_limit_bytes=44 * 1024 * 1024
        ),
        name="state_space_layer",
    )(
        *[
            pltpu.with_memory_space_constraint(a, pltpu.HBM)
            for a in (
                x_in, b_in, step_size.T, log_decay.T, skip.reshape(1, HEADS), norm_gain.reshape(1, CHAN),
                gate_z, c_in, out_weight,
            )
        ]
    )


def solution(mesh):
    placed = (
        P("ctx", "tp"),
        P("ctx", "tp"),
        P("ctx", "tp"),
        P("ctx", "tp"),
        P("ctx", "tp"),
        P("ctx", "tp"),
        P("tp"),
        P("tp"),
        P("tp", None),
    )
    return jax.shard_map(
        on_device, mesh=mesh, in_specs=placed, out_specs=P(("ctx", "tp"), None), check_vma=False
    )
```
